256 devices in a mesh: gx: 32 (over y, z), gy: 8 (over x, core).
Axes of the slice: x: 4, y: 4, z: 8, core: 2. Of those that a mesh axis runs over, the one named last changes fastest.
Arguments:
- features: bfloat16 [2048, 64, 512], P(('gx', 'gy')), may hold values from -6 to 6
- neighbours: int32 [2048, 6], P(('gx', 'gy')), may hold values from 0 to 16, as said below
- counts: int32 [256], P(('gx', 'gy')), may hold values from 1 to 8, as said below
- conv_weight: bfloat16 [64, 448], replicated, may hold values from -0.25 to 0.25
- down_weight: bfloat16 [128, 512], replicated, may hold values from -0.25 to 0.25
- head_weight: bfloat16 [128, 128], replicated, may hold values from -0.5 to 0.5
- coarse_map: int32 [256, 8], P(('gx', 'gy')), may hold values from 0 to 32, as said below
- latent_grad: bfloat16 [256, 512, 128], P(('gx', 'gy')), may hold values from -6 to 6
Outputs:
- latent: bfloat16 [256, 512, 128], P(('gx', 'gy'))
- features_grad: bfloat16 [2048, 64, 512], P(('gx', 'gy'))
- conv_grad: float32 [64, 448], replicated
- down_grad: float32 [128, 512], replicated
- head_grad: float32 [128, 128], replicated
The draws below stay inside these ranges and needn't reach their ends.
Inputs may be any that keep to these rules, and one draw needn't show every extreme that they name: `counts`: in every draw, max(1, (devices along gx times devices along gy) // 8) columns have exactly 8 active blocks; each other column has between 1 and 4. 16 means no neighbour; a value below 8 is an active slot of the same column; a value v of 8 or more is the active slot v - 8 of the adjacent column in that direction; the z directions never name another column; inactive slots have no neighbours. `coarse_map`: 32 marks an empty octant; every other entry names an active block's octant, and each such octant is named at most once among the four columns that share a merged list.
All inputs are finite; a program needn't handle non-finite values.
Results may differ from the reference program's by a relative error of at most 0.013.
Values may be sent and summed in bfloat16 or wider, within the bound.
A program may use at most 128 MiB of HBM per device.

```python
import jax
import jax.numpy as jnp
from jax import lax

C1 = 64
C2 = 128
NB = 8
NC = 1
BLOCKS = 2048
CBLOCKS = 256
N_GX = 32
N_GY = 8


def group_counts(key):
    devices = N_GX * N_GY
    base = jax.random.randint(jax.random.fold_in(key, 101), (devices,), NB // 8, NB // 2 + 1)
    order = jax.random.permutation(jax.random.fold_in(key, 102), devices)
    return jnp.where(order < max(1, devices // 8), NB, base).astype(jnp.int32)


def draw_counts(key, part):
    return group_counts(key)


def draw_neighbours(key, part):
    devices = N_GX * N_GY
    counts = group_counts(key)
    blocks = jnp.arange(devices * NB)
    column = blocks // NB
    slots = blocks % NB
    column_x = column // N_GY
    column_y = column % N_GY
    is_live = slots < counts[column]
    empty = 2 * NB
    offsets = ((-N_GY, column_x > 0), (N_GY, column_x < N_GX - 1), (-1, column_y > 0), (1, column_y < N_GY - 1))
    entries = []
    for direction in range(6):
        dir_key = jax.random.fold_in(key, 200 + direction)
        category = jax.random.randint(jax.random.fold_in(dir_key, 1), (devices * NB,), 0, 10)
        nearby = jax.random.randint(jax.random.fold_in(dir_key, 2), (devices * NB,), 0, counts[column])
        if direction < 4:
            other = jnp.clip(column + offsets[direction][0], 0, devices - 1)
            remote = NB + jax.random.randint(jax.random.fold_in(dir_key, 3), (devices * NB,), 0, counts[other])
            entry_value = jnp.where(category < 4, nearby, jnp.where((category < 8) & offsets[direction][1], remote, empty))
        else:
            entry_value = jnp.where(category < 7, nearby, empty)
        entries.append(jnp.where(is_live, entry_value, empty))
    return jnp.stack(entries, axis=1).astype(jnp.int32)


def draw_coarse_map(key, part):
    counts = group_counts(key)
    half_x = N_GX // 2
    half_y = N_GY // 2
    groups = half_x * half_y
    octant_total = 4 * NB
    octant_ids = jnp.arange(octant_total)
    member = octant_ids // NB
    slots = octant_ids % NB
    member_x = member // 2
    member_y = member % 2

    def one_group(group_index, group_key):
        start_x = 2 * (group_index // half_y)
        start_y = 2 * (group_index % half_y)
        column = (start_x + member_x) * N_GY + start_y + member_y
        is_live = slots < counts[column]
        order_rank = jnp.cumsum(is_live.astype(jnp.int32)) - 1
        places = jax.random.permutation(group_key, octant_total)
        target = jnp.where(is_live, places[jnp.clip(order_rank, 0, octant_total - 1)], octant_total)
        owner = target // (NC * 8)
        relation = (member_x ^ owner // 2) + 2 * (member_y ^ owner % 2)
        entry_value = (relation * NB + slots).astype(jnp.int32)
        lookup = jnp.full((octant_total + 1,), 4 * NB, jnp.int32).at[target].set(entry_value)
        return lookup[:octant_total]
    group_keys = jax.random.split(jax.random.fold_in(key, 300), groups)
    tables = jax.vmap(one_group)(jnp.arange(groups), group_keys)
    tables = tables.reshape(half_x, half_y, 2, 2, NC, 8).transpose(0, 2, 1, 3, 4, 5)
    return tables.reshape(N_GX * N_GY * NC, 8).astype(jnp.int32)


def levels(own_key, extent, cuts, smallest, largest):
    def one(position, blocks):
        heights = jax.random.uniform(jax.random.fold_in(jax.random.fold_in(own_key, 6), position), (blocks,), jnp.float32, smallest / len(cuts), largest / len(cuts))
        return jnp.repeat(jnp.exp(heights), extent[position] // blocks).reshape((-1,) + (1,) * (len(extent) - position - 1))

    level = one(*cuts[0])
    for cut in cuts[1:]:
        level = level * one(*cut)
    return level


def bell_draw(rng, dims, scale, limit, shards=(), kind=jnp.bfloat16):
    array = jax.random.normal(rng, dims, jnp.float32) * scale
    if len(shards) > 0:
        array = levels(rng, dims, shards, -0.22, 0.18) * array
    return jnp.clip(array, min=-limit, max=limit).astype(kind)


def setup_inputs(seed: int = 0) -> dict:
    splits = jax.random.split(jax.random.key(seed), 9)
    return {
        "features": bell_draw(splits[0], (BLOCKS, C1, 512), 1.0, 6.0, ((0, 256),)),
        "neighbours": draw_neighbours(jax.random.fold_in(splits[8], 71), 0),
        "counts": draw_counts(jax.random.fold_in(splits[8], 71), 0),
        "conv_weight": bell_draw(splits[3], (C1, 7 * C1), (7 * C1) ** -0.5, 0.25),
        "down_weight": bell_draw(splits[4], (C2, 8 * C1), (8 * C1) ** -0.5, 0.25),
        "head_weight": bell_draw(splits[5], (C2, C2), C2 ** -0.5, 0.5),
        "coarse_map": draw_coarse_map(jax.random.fold_in(splits[8], 71), 0),
        "latent_grad": bell_draw(splits[7], (CBLOCKS, 512, C2), 1.0, 6.0, ((0, 256),)),
    }


def silu_grad(values):
    sigmoid_value = jax.nn.sigmoid(values)
    return sigmoid_value * (1.0 + values * (1.0 - sigmoid_value))

def face_layers(volume):
    number, channels = (volume.shape[0], volume.shape[1])

    def flatten(plane):
        return plane.reshape(number, channels * 64)
    return (flatten(volume[:, :, 7]), flatten(volume[:, :, 0]), flatten(volume[:, :, :, 7]), flatten(volume[:, :, :, 0]), flatten(volume[:, :, :, :, 7]), flatten(volume[:, :, :, :, 0]))

def pick_rows(local_rows, remote_rows, index):
    width = local_rows.shape[1]
    pooled = jnp.concatenate([local_rows, remote_rows, jnp.zeros((1, width), local_rows.dtype)], axis=0)
    return pooled[index]

def neighbour_stack(volume, remotes, links):
    number, channels = (volume.shape[0], volume.shape[1])
    faces = face_layers(volume)
    blank = jnp.zeros_like(faces[4])
    sources = (remotes[0], remotes[1], remotes[2], remotes[3], blank, blank)
    picked = [pick_rows(faces[direction], sources[direction], links[:, direction]).reshape(number, channels, 8, 8) for direction in range(6)]
    x_minus = jnp.concatenate([picked[0][:, :, None], volume[:, :, :7]], axis=2)
    x_plus = jnp.concatenate([volume[:, :, 1:], picked[1][:, :, None]], axis=2)
    y_minus = jnp.concatenate([picked[2][:, :, :, None], volume[:, :, :, :7]], axis=3)
    y_plus = jnp.concatenate([volume[:, :, :, 1:], picked[3][:, :, :, None]], axis=3)
    z_minus = jnp.concatenate([picked[4][..., None], volume[..., :7]], axis=4)
    z_plus = jnp.concatenate([volume[..., 1:], picked[5][..., None]], axis=4)
    joined = jnp.concatenate([volume, x_minus, x_plus, y_minus, y_plus, z_minus, z_plus], axis=1)
    return joined.reshape(number, 7 * channels, 512)

def stack_grad(taps_grad, links):
    number, channels = (taps_grad.shape[0], taps_grad.shape[1] // 7)
    parts = taps_grad.reshape(number, 7, channels, 8, 8, 8)
    grad_volume = parts[:, 0]
    grad_volume = grad_volume + jnp.pad(parts[:, 1, :, 1:], ((0, 0), (0, 0), (0, 1), (0, 0), (0, 0)))
    grad_volume = grad_volume + jnp.pad(parts[:, 2, :, :7], ((0, 0), (0, 0), (1, 0), (0, 0), (0, 0)))
    grad_volume = grad_volume + jnp.pad(parts[:, 3, :, :, 1:], ((0, 0), (0, 0), (0, 0), (0, 1), (0, 0)))
    grad_volume = grad_volume + jnp.pad(parts[:, 4, :, :, :7], ((0, 0), (0, 0), (0, 0), (1, 0), (0, 0)))
    grad_volume = grad_volume + jnp.pad(parts[:, 5, :, :, :, 1:], ((0, 0), (0, 0), (0, 0), (0, 0), (0, 1)))
    grad_volume = grad_volume + jnp.pad(parts[:, 6, :, :, :, :7], ((0, 0), (0, 0), (0, 0), (0, 0), (1, 0)))
    face_grads = (parts[:, 1, :, 0], parts[:, 2, :, 7], parts[:, 3, :, :, 0], parts[:, 4, :, :, 7], parts[:, 5, :, :, :, 0], parts[:, 6, :, :, :, 7])
    pools = [jnp.zeros((2 * number + 1, channels * 64), jnp.float32).at[links[:, direction]].add(face_grads[direction].reshape(number, channels * 64)) for direction in range(6)]
    shaped = [pools[direction][:number].reshape(number, channels, 8, 8) for direction in range(6)]
    grad_volume = grad_volume.at[:, :, 7].add(shaped[0])
    grad_volume = grad_volume.at[:, :, 0].add(shaped[1])
    grad_volume = grad_volume.at[:, :, :, 7].add(shaped[2])
    grad_volume = grad_volume.at[:, :, :, 0].add(shaped[3])
    grad_volume = grad_volume.at[:, :, :, :, 7].add(shaped[4])
    grad_volume = grad_volume.at[:, :, :, :, 0].add(shaped[5])
    far_rows = jnp.stack([pools[direction][number:2 * number] for direction in range(4)]).astype(jnp.bfloat16)
    return (grad_volume, far_rows)

def add_faces(grad_volume, into_xhigh, into_xlow, into_yhigh, into_ylow):
    number, channels = (grad_volume.shape[0], grad_volume.shape[1])

    def planes(rows):
        return rows.astype(jnp.float32).reshape(number, channels, 8, 8)
    grad_volume = grad_volume.at[:, :, 7].add(planes(into_xhigh))
    grad_volume = grad_volume.at[:, :, 0].add(planes(into_xlow))
    grad_volume = grad_volume.at[:, :, :, 7].add(planes(into_yhigh))
    grad_volume = grad_volume.at[:, :, :, 0].add(planes(into_ylow))
    return grad_volume

def to_patches(volume):
    number, channels = (volume.shape[0], volume.shape[1])
    split = volume.reshape(number, channels, 4, 2, 4, 2, 4, 2).transpose(0, 1, 3, 5, 7, 2, 4, 6)
    return split.reshape(number, channels * 8, 64)

def from_patches(patch):
    number, channels = (patch.shape[0], patch.shape[1] // 8)
    split = patch.reshape(number, channels, 2, 2, 2, 4, 4, 4).transpose(0, 1, 5, 2, 6, 3, 7, 4)
    return split.reshape(number, channels, 512)

def shift_grid(values, axis_number, steps):
    grid = values.reshape(N_GX, N_GY, NB, values.shape[-1])
    length = grid.shape[axis_number]
    first = lax.slice_in_dim(grid, 0, 1, axis=axis_number)
    if steps == 1:
        moved = jnp.concatenate([jnp.zeros_like(first), lax.slice_in_dim(grid, 0, length - 1, axis=axis_number)], axis=axis_number)
    else:
        moved = jnp.concatenate([lax.slice_in_dim(grid, 1, length, axis=axis_number), jnp.zeros_like(first)], axis=axis_number)
    return moved.reshape(values.shape)

def reference(features, neighbours, counts, conv_weight, down_weight, head_weight, coarse_map, latent_grad):
    devices = N_GX * N_GY
    slot_owner = jnp.arange(BLOCKS) // NB
    active = jnp.arange(BLOCKS) % NB < counts[slot_owner]
    masked_parity = jnp.where(active[:, None, None], features, jnp.zeros((), jnp.bfloat16))
    masked = from_patches(masked_parity.reshape(BLOCKS, C1 * 8, 64))
    faces = face_layers(masked.reshape(BLOCKS, C1, 8, 8, 8))
    remotes = (shift_grid(faces[0], 0, 1), shift_grid(faces[1], 0, -1), shift_grid(faces[2], 1, 1), shift_grid(faces[3], 1, -1))
    conv_f = conv_weight.astype(jnp.float32)
    down_f = down_weight.astype(jnp.float32)
    head_f = head_weight.astype(jnp.float32)

    def per_device(values):
        return values.reshape((devices, values.shape[0] // devices) + values.shape[1:])

    def level_one(items):
        local_rows, remote_a, remote_b, remote_c, remote_d, links = items
        taps = neighbour_stack(local_rows.reshape(NB, C1, 8, 8, 8), (remote_a, remote_b, remote_c, remote_d), links)
        hidden = jnp.einsum('ok,bkv->bov', conv_f, taps.astype(jnp.float32))
        act = jax.nn.silu(hidden).astype(jnp.bfloat16)
        return (taps, hidden, act)

    def forward_one(items):
        taps, hidden, act = level_one(items)
        octants = jnp.einsum('ok,bkv->bvo', down_f, to_patches(act).astype(jnp.float32)).astype(jnp.bfloat16)
        return octants.reshape(NB, 64 * C2)
    level_inputs = (per_device(masked), per_device(remotes[0]), per_device(remotes[1]), per_device(remotes[2]), per_device(remotes[3]), per_device(neighbours))
    octants = lax.map(forward_one, level_inputs)
    grid = octants.reshape(N_GX // 2, 2, N_GY // 2, 2, NB, 64 * C2)
    across_x = jnp.flip(grid, 1)
    across_y = jnp.flip(grid, 3)
    across_both = jnp.flip(across_x, 3)
    merged = jnp.concatenate([grid, across_x, across_y, across_both], axis=4).reshape(devices, 4 * NB, 64 * C2)

    def coarse_one(items):
        merged_rows, links, grad_rows = items
        padded = jnp.concatenate([merged_rows, jnp.zeros((1, 64 * C2), jnp.bfloat16)], axis=0)
        coarse = padded[links].reshape(NC, 512, C2)
        coarse_act = jax.nn.silu(coarse.astype(jnp.float32)).astype(jnp.bfloat16)
        latent = jnp.einsum('oi,cvi->cvo', head_f, coarse_act.astype(jnp.float32)).astype(jnp.bfloat16)
        grad_f = grad_rows.astype(jnp.float32)
        act_grad = jnp.einsum('oi,cvo->cvi', head_f, grad_f)
        coarse_grad = (act_grad * silu_grad(coarse.astype(jnp.float32))).astype(jnp.bfloat16)
        head_part = jnp.einsum('cvo,cvi->oi', grad_f, coarse_act.astype(jnp.float32))
        back_rows = jnp.zeros((4 * NB + 1, 64 * C2), jnp.float32).at[links.reshape(-1)].add(coarse_grad.reshape(NC * 8, 64 * C2).astype(jnp.float32))
        return (latent, back_rows[:4 * NB].astype(jnp.bfloat16), head_part)
    latent, merged_grad, head_parts = lax.map(coarse_one, (merged, per_device(coarse_map), per_device(latent_grad)))
    back = merged_grad.astype(jnp.float32).reshape(N_GX // 2, 2, N_GY // 2, 2, 4, NB, 64 * C2)
    octant_grad = back[:, :, :, :, 0] + jnp.flip(back[:, :, :, :, 1], 1) + jnp.flip(back[:, :, :, :, 2], 3) + jnp.flip(jnp.flip(back[:, :, :, :, 3], 1), 3)
    octant_grad = octant_grad.astype(jnp.bfloat16).reshape(devices, NB, 64, C2)

    def backward_one(items):
        level_items, grad_octant = items
        taps, hidden, act = level_one(level_items)
        grad_f = grad_octant.astype(jnp.float32)
        down_part = jnp.einsum('bvo,bkv->ok', grad_f, to_patches(act).astype(jnp.float32))
        patch_grad = jnp.einsum('ok,bvo->bkv', down_f, grad_f)
        hidden_grad = (from_patches(patch_grad) * silu_grad(hidden)).astype(jnp.bfloat16)
        conv_part = jnp.einsum('bov,bkv->ok', hidden_grad.astype(jnp.float32), taps.astype(jnp.float32))
        taps_grad = jnp.einsum('ok,bov->bkv', conv_f, hidden_grad.astype(jnp.float32))
        near_grad, far_rows = stack_grad(taps_grad, level_items[5])
        return (near_grad, far_rows, conv_part, down_part)
    near_grad, far_rows, conv_parts, down_parts = lax.map(backward_one, (level_inputs, octant_grad))
    into_xhigh = shift_grid(far_rows[:, 0].reshape(BLOCKS, C1 * 64), 0, -1)
    into_xlow = shift_grid(far_rows[:, 1].reshape(BLOCKS, C1 * 64), 0, 1)
    into_yhigh = shift_grid(far_rows[:, 2].reshape(BLOCKS, C1 * 64), 1, -1)
    into_ylow = shift_grid(far_rows[:, 3].reshape(BLOCKS, C1 * 64), 1, 1)

    def final_one(items):
        grad_volume, part_a, part_b, part_c, part_d, active_rows = items
        total = add_faces(grad_volume, part_a, part_b, part_c, part_d).reshape(NB, C1, 512)
        total = to_patches(total).reshape(NB, C1, 512)
        return jnp.where(active_rows[:, None, None], total, 0.0).astype(jnp.bfloat16)
    features_grad = lax.map(final_one, (near_grad, per_device(into_xhigh), per_device(into_xlow), per_device(into_yhigh), per_device(into_ylow), per_device(active)))
    scale = float(BLOCKS) ** (-0.5)
    return (latent.reshape(CBLOCKS, 512, C2), features_grad.reshape(BLOCKS, C1, 512), lax.optimization_barrier(jnp.sum(conv_parts, axis=0)) * scale, lax.optimization_barrier(jnp.sum(down_parts, axis=0)) * scale, lax.optimization_barrier(jnp.sum(head_parts, axis=0)) * scale)
```

```python
import jax
import jax.numpy as jnp
from jax import lax
from jax.experimental import pallas as pl
from jax.experimental.pallas import tpu as pltpu
from jax.sharding import PartitionSpec as P

MESH = pl.DeviceIdType.MESH
F32 = jnp.float32
BF16 = jnp.bfloat16
STRIDE = (16, 4, 1)
GRAD_ROWS = 1024


def ring_z(n_gx):
    return 8 if n_gx % 8 == 0 else n_gx // 2


def dot(a, b, ca, cb):
    return lax.dot_general(a, b, (((ca,), (cb,)), ((), ())), preferred_element_type=F32)


def lanes():
    return lax.broadcasted_iota(jnp.int32, (64, 128), 1)


def flag(value):
    return jnp.broadcast_to(value, (64, 128))


def roll(values, amount):
    amount = amount % 128
    return values if amount == 0 else pltpu.roll(values, amount, 1)


def column(axis, bit, s):
    high, low = s // 2, s % 2
    bits = [high, low]
    bits.insert(axis, bit)
    return bits[0] * 4 + bits[1] * 2 + bits[2]


def field(axis):
    return lax.rem(lax.div(lanes(), STRIDE[axis]), 4)


def pack_face(cols, axis, upper):
    step = STRIDE[axis]
    place = field(axis)
    out = None
    for s in range(4):
        shift = step * (s - 3) if upper else step * s
        moved = roll(cols[column(axis, int(upper), s)], shift)
        out = moved if out is None else jnp.where(place == s, moved, out)
    return out


def shift_minus(cols, axis, face):
    step = STRIDE[axis]
    edge = field(axis) == 0
    out = [None] * 8
    for s in range(4):
        low, high = column(axis, 0, s), column(axis, 1, s)
        out[high] = cols[low]
        out[low] = jnp.where(edge, roll(face, -step * s), roll(cols[high], step))
    return out


def shift_plus(cols, axis, face):
    step = STRIDE[axis]
    edge = field(axis) == 3
    out = [None] * 8
    for s in range(4):
        low, high = column(axis, 0, s), column(axis, 1, s)
        out[low] = cols[high]
        out[high] = jnp.where(edge, roll(face, step * (3 - s)), roll(cols[low], -step))
    return out


def sigmoid(values):
    return 1.0 / (1.0 + jnp.exp(-values))


def silu_grad(values):
    s = sigmoid(values)
    return s * (1.0 + values * (1.0 - s))


def edges(n_gx, n_gy):
    x, y = lax.axis_index("gx"), lax.axis_index("gy")
    return (x == 0, x == n_gx - 1, y == 0, y == n_gy - 1)


def link_of(links, slot, direction, rim):
    value = links[slot, direction]
    if direction < 4:
        return jnp.where(jnp.logical_and(rim[direction], value >= 8), 16, value)
    return value


def selection():
    row = lax.broadcasted_iota(jnp.int32, (512, 512), 0)
    col = lax.broadcasted_iota(jnp.int32, (512, 512), 1)
    return jnp.where(col == lax.rem(row, 64) * 8 + lax.div(row, 64), 1.0, 0.0).astype(BF16)


def pack_kernel(counts, maps, features, down, cube, faces, down_rows, map_out):
    low_half = lanes() < 64
    zero = jnp.zeros((64, 128), BF16)

    def pair(i, carry):
        keep_a = flag(counts[0] - 2 * i) > 0
        keep_b = flag(counts[0] - 2 * i) > 1
        cols = [None] * 8
        for pq in range(4):
            a = jnp.where(keep_a, features[2 * i, :, pq * 128 : pq * 128 + 128], zero)
            b = jnp.where(keep_b, features[2 * i + 1, :, pq * 128 : pq * 128 + 128], zero)
            cols[2 * pq] = jnp.where(low_half, a, roll(b, 64))
            cols[2 * pq + 1] = jnp.where(low_half, roll(a, 64), b)
        for c in range(8):
            cube[i, :, c * 128 : c * 128 + 128] = cols[c]
        for d in range(6):
            faces[d, i] = pack_face(cols, d // 2, d % 2 == 0)
        return carry

    lax.fori_loop(0, 4, pair, 0)
    down_rows[...] = dot(selection(), down[...], 1, 1).astype(BF16)
    lane = lax.broadcasted_iota(jnp.int32, (8, 128), 1)
    table = jnp.zeros((8, 128), jnp.int32)
    for k in range(8):
        table = jnp.where(lane == k, jnp.broadcast_to(maps[0, k], (8, 128)), table)
    map_out[...] = table


def level_kernel(n_gx, n_gy, links, cube, faces, remote, conv, down_rows, taps, hidden, act, octants, pool):
    rim = edges(n_gx, n_gy)
    low_half = lanes() < 64
    zero = jnp.zeros((64, 128), BF16)
    for d in range(6):
        pool[d, 0, 8] = zero
        pool[d, 1, 8] = zero

    def fill(j, carry):
        for d in range(6):
            own = faces[d, j]
            pool[d, 0, j] = own
            pool[d, 1, j] = roll(own, 64)
            far = remote[d, j] if d < 4 else zero
            pool[d, 0, 4 + j] = far
            pool[d, 1, 4 + j] = roll(far, 64) if d < 4 else far
        return carry

    lax.fori_loop(0, 4, fill, 0)

    def pair(i, carry):
        cols = [cube[i, :, c * 128 : c * 128 + 128] for c in range(8)]
        for c in range(8):
            taps[i, 0:64, c * 128 : c * 128 + 128] = cols[c]
        for d in range(6):
            e0 = link_of(links, 2 * i, d, rim)
            e1 = link_of(links, 2 * i + 1, d, rim)
            face = jnp.where(
                low_half,
                pool[d, lax.rem(e0, 2), lax.div(e0, 2)],
                pool[d, 1 - lax.rem(e1, 2), lax.div(e1, 2)],
            )
            moved = (shift_minus if d % 2 == 0 else shift_plus)(cols, d // 2, face)
            for c in range(8):
                taps[i, 64 * (d + 1) : 64 * (d + 2), c * 128 : c * 128 + 128] = moved[c]
        values = dot(conv[...], taps[i], 1, 0)
        hidden[i] = values
        active = (values * sigmoid(values)).astype(BF16)
        for c in range(8):
            act[i, c * 64 : c * 64 + 64, :] = active[:, c * 128 : c * 128 + 128]
        rows = dot(act[i], down_rows[...], 0, 0).astype(BF16)
        octants[2 * i] = rows[:64]
        octants[2 * i + 1] = rows[64:]
        return carry

    lax.fori_loop(0, 4, pair, 0)


def coarse_kernel(maps, own, received, head, grad_in, latent, coarse_grad, head_sum, coarse):
    zero = jnp.zeros((64, 128), BF16)
    for k in range(8):
        e = maps[0, k]
        mine = own[jnp.minimum(e, 7)]
        other = received[jnp.clip(e - 8, 0, 23)]
        row = jnp.where(flag(e) < 8, mine, jnp.where(flag(e) < 32, other, zero))
        coarse[k * 64 : k * 64 + 64, :] = row
    values = coarse[...].astype(F32)
    s = sigmoid(values)
    active = (values * s).astype(BF16)
    latent[0] = dot(active, head[...], 1, 1).astype(BF16)
    grad = grad_in[0]
    back = dot(grad, head[...], 1, 0) * (s * (1.0 + values * (1.0 - s)))
    back = back.astype(BF16)
    for k in range(8):
        coarse_grad[k] = back[k * 64 : k * 64 + 64]
    head_sum[...] = dot(grad, active, 0, 0).astype(BF16)


def backward_kernel(
    n_gx, n_gy, links, maps, far_maps, own, received, hidden, act, taps, down_rows, head_sum,
    grads, hidden_grad, near_faces, far_faces, inverse, pool, conv_acc, down_acc,
):
    rim = edges(n_gx, n_gy)
    lane = lanes()
    zero = jnp.zeros((64, 128), BF16)
    for s in range(8):
        inverse[s] = 32
    for m in range(4):
        for k in range(8):
            e = maps[0, k] if m == 0 else far_maps[m - 1, 0, k]
            slot = lax.rem(e, 8)
            inverse[slot] = jnp.where(lax.div(e, 8) == m, m * 8 + k, inverse[slot])
    for d in range(6):
        for j in range(9):
            pool[d, j] = jnp.zeros((64, 128), F32)
    conv_acc[...] = jnp.zeros_like(conv_acc)
    down_acc[...] = jnp.zeros_like(down_acc)

    def row_of(slot):
        e = inverse[slot]
        mine = own[jnp.minimum(e, 7)]
        other = received[jnp.clip(e - 8, 0, 23)]
        return jnp.where(flag(e) < 8, mine, jnp.where(flag(e) < 32, other, zero))

    def pair(i, carry):
        rows = jnp.concatenate([row_of(2 * i), row_of(2 * i + 1)], axis=0)
        down_acc[...] += dot(act[i], rows, 1, 0)
        patch = dot(down_rows[...], rows, 1, 1)
        cols = []
        for c in range(8):
            slope = silu_grad(hidden[i, :, c * 128 : c * 128 + 128])
            value = (patch[c * 64 : c * 64 + 64] * slope).astype(BF16)
            hidden_grad[i, :, c * 128 : c * 128 + 128] = value
            cols.append(value)
        conv_acc[...] += dot(hidden_grad[i], taps[i], 1, 1)
        for d in range(6):
            face = pack_face(cols, d // 2, d % 2 == 1).astype(F32)
            swapped = roll(face, 64)
            for g in range(2):
                e = link_of(links, 2 * i + g, d, rim)
                half = lax.rem(e, 2)
                row = lax.div(e, 2)
                value = jnp.where(flag(half) == g, face, swapped)
                value = jnp.where(lax.div(lane, 64) == flag(half), value, 0.0)
                pool[d, row] = pool[d, row] + value
        return carry

    lax.fori_loop(0, 4, pair, 0)
    for d in range(6):
        for j in range(4):
            near_faces[d, j] = pool[d, j]
            if d < 4:
                far_faces[d, j] = pool[d, 4 + j].astype(BF16)
    wide = conv_acc[...].astype(BF16)
    for j in range(3):
        grads[j * 64 : j * 64 + 64, :] = wide[:, j * 128 : j * 128 + 128]
    grads[192:256, :] = jnp.concatenate([wide[:, 384:448], jnp.zeros((64, 64), BF16)], axis=1)
    ordered = dot(down_acc[...].astype(BF16), selection(), 0, 0).astype(BF16)
    for j in range(4):
        grads[256 + j * 128 : 384 + j * 128, :] = ordered[:, j * 128 : j * 128 + 128]
    grads[768:896, :] = head_sum[...]
    grads[896:1024, :] = jnp.zeros((128, 128), BF16)


def final_kernel(counts, conv, hidden_grad, near_faces, far_in, out, turned, taps):
    low_half = lanes() < 64
    zero = jnp.zeros((64, 128), F32)
    for d in range(7):
        block = conv[:, d * 64 : d * 64 + 64].astype(F32)
        turned[:, d * 64 : d * 64 + 64] = block.T.astype(BF16)

    def pair(i, carry):
        cols = [hidden_grad[i, :, c * 128 : c * 128 + 128] for c in range(8)]
        for c in range(8):
            taps[0:64, c * 128 : c * 128 + 128] = cols[c]
        for d in range(6):
            face = near_faces[d, i]
            if d < 4:
                face = face + far_in[d, i].astype(F32)
            moved = (shift_plus if d % 2 == 0 else shift_minus)(cols, d // 2, face.astype(BF16))
            for c in range(8):
                taps[64 * (d + 1) : 64 * (d + 2), c * 128 : c * 128 + 128] = moved[c]
        total = dot(turned[...], taps[...], 1, 0)
        keep_a = flag(counts[0] - 2 * i) > 0
        keep_b = flag(counts[0] - 2 * i) > 1
        for pq in range(4):
            even = total[:, pq * 256 : pq * 256 + 128]
            odd = total[:, pq * 256 + 128 : pq * 256 + 256]
            a = jnp.where(low_half, even, roll(odd, 64))
            b = jnp.where(low_half, roll(even, 64), odd)
            out[2 * i, :, pq * 128 : pq * 128 + 128] = jnp.where(keep_a, a, zero).astype(BF16)
            out[2 * i + 1, :, pq * 128 : pq * 128 + 128] = jnp.where(keep_b, b, zero).astype(BF16)
        return carry

    lax.fori_loop(0, 4, pair, 0)


def greet(devices):
    barrier = pltpu.get_barrier_semaphore()
    for device in devices:
        pl.semaphore_signal(barrier, inc=1, device_id=device, device_id_type=MESH)
    pl.semaphore_wait(barrier, len(devices))


def around(n_gx, n_gy):
    x, y = lax.axis_index("gx"), lax.axis_index("gy")
    return (
        (lax.rem(x + 1, n_gx), y),
        (lax.rem(x + n_gx - 1, n_gx), y),
        (x, lax.rem(y + 1, n_gy)),
        (x, lax.rem(y + n_gy - 1, n_gy)),
    )


def partners():
    x, y = lax.axis_index("gx"), lax.axis_index("gy")
    x1 = x + 1 - 2 * lax.rem(x, 2)
    y1 = y + 1 - 2 * lax.rem(y, 2)
    return ((x1, y), (x, y1), (x1, y1))


def run_copies(copies):
    for copy in copies:
        copy.start()
    for copy in copies:
        copy.wait()


def faces_kernel(n_gx, n_gy, faces, table, far, tables, send, recv):
    beside = around(n_gx, n_gy)
    merged = partners()
    greet(beside + (merged[2],))
    copies = []
    for d in range(4):
        copies.append(pltpu.make_async_remote_copy(
            src_ref=faces.at[d], dst_ref=far.at[d], send_sem=send.at[d], recv_sem=recv.at[d],
            device_id=beside[d], device_id_type=MESH,
        ))
    for m in range(3):
        copies.append(pltpu.make_async_remote_copy(
            src_ref=table, dst_ref=tables.at[m], send_sem=send.at[4 + m], recv_sem=recv.at[4 + m],
            device_id=merged[m], device_id_type=MESH,
        ))
    run_copies(copies)


def return_kernel(n_gx, n_gy, faces, far, send, recv):
    beside = around(n_gx, n_gy)
    greet(beside)
    target = (beside[1], beside[0], beside[3], beside[2])
    run_copies([
        pltpu.make_async_remote_copy(
            src_ref=faces.at[d], dst_ref=far.at[d], send_sem=send.at[d], recv_sem=recv.at[d],
            device_id=target[d], device_id_type=MESH,
        )
        for d in range(4)
    ])


def merge_kernel(own, received, send, recv):
    merged = partners()
    greet(merged)
    run_copies([
        pltpu.make_async_remote_copy(
            src_ref=own, dst_ref=received.at[pl.ds(8 * m, 8)], send_sem=send.at[m],
            recv_sem=recv.at[m], device_id=merged[m], device_id_type=MESH,
        )
        for m in range(3)
    ])


def sum_kernel(
    n_gx, n_gy, grads, conv_out, down_out, head_out,
    part_a, sum_a, part_b, sum_b, part_c, part_d, part_e,
    send_a, recv_a, send_b, recv_b, send_c, recv_c, send_d, recv_d, send_e, recv_e,
):
    nz = ring_z(n_gx)
    ny = n_gx // nz
    x, me = lax.axis_index("gx"), lax.axis_index("gy")
    y, z = lax.div(x, nz), lax.rem(x, nz)
    scale = float(2048) ** -0.5
    rows_g = [(x, lax.rem(me + k, n_gy)) for k in range(1, n_gy)]
    rows_z = [(y * nz + lax.rem(z + k, nz), me) for k in range(1, nz)]
    rows_y = [(lax.rem(y + k, ny) * nz + z, me) for k in range(1, ny)]
    greet(rows_g + rows_z + rows_y)

    def send(source, target, sems, k, device):
        return pltpu.make_async_remote_copy(
            src_ref=source, dst_ref=target, send_sem=sems[0].at[k], recv_sem=sems[1].at[k],
            device_id=device, device_id_type=MESH,
        )

    copies = [
        send(grads.at[lax.rem(me + k, n_gy)], part_a.at[k], (send_a, recv_a), k, rows_g[k - 1])
        for k in range(1, n_gy)
    ]
    run_copies(copies)
    total = grads[me].astype(F32)
    for k in range(1, n_gy):
        total = total + part_a[k].astype(F32)
    sum_a[...] = total.astype(BF16)
    copies = [
        send(sum_a.at[lax.rem(z + k, nz)], part_b.at[k], (send_b, recv_b), k, rows_z[k - 1])
        for k in range(1, nz)
    ]
    run_copies(copies)
    total = sum_a[z].astype(F32)
    for k in range(1, nz):
        total = total + part_b[k].astype(F32)
    sum_b[...] = total
    part_c[y] = total
    copies = [
        send(sum_b, part_c.at[y], (send_c, recv_c), k, rows_y[k - 1]) for k in range(1, ny)
    ]
    run_copies(copies)
    total = part_c[0]
    for k in range(1, ny):
        total = total + part_c[k]
    part_d[z] = total.astype(BF16)
    copies = [
        send(part_d.at[z], part_d.at[z], (send_d, recv_d), k, rows_z[k - 1]) for k in range(1, nz)
    ]
    run_copies(copies)
    part_e[me] = part_d[...]
    copies = [
        send(part_d, part_e.at[me], (send_e, recv_e), k, rows_g[k - 1]) for k in range(1, n_gy)
    ]
    run_copies(copies)
    result = part_e[...].reshape(GRAD_ROWS, 128).astype(F32) * scale
    for j in range(3):
        conv_out[:, j * 128 : j * 128 + 128] = result[j * 64 : j * 64 + 64]
    conv_out[:, 384:448] = result[192:256, :64]
    for j in range(4):
        down_out[:, j * 128 : j * 128 + 128] = result[256 + j * 128 : 384 + j * 128]
    head_out[...] = result[768:896]


VM = pl.BlockSpec(memory_space=pltpu.VMEM)
SM = pl.BlockSpec(memory_space=pltpu.SMEM)
ANY = pl.BlockSpec(memory_space=pl.ANY)
DMA = pltpu.SemaphoreType.DMA


def shape(*dims, dtype=BF16):
    return jax.ShapeDtypeStruct(dims, dtype)


def call(kernel, name, ins, outs, shapes, scratch=(), channel=None):
    if channel is None:
        params = pltpu.CompilerParams()
    else:
        params = pltpu.CompilerParams(collective_id=channel, has_side_effects=True)
    return pl.pallas_call(
        kernel, name=name, in_specs=ins, out_specs=outs, out_shape=shapes,
        scratch_shapes=list(scratch), compiler_params=params,
    )


def bind(kernel, *fixed):
    def run(*refs):
        kernel(*fixed, *refs)

    return run


def body(
    features, neighbours, counts, conv_weight, down_weight, head_weight, coarse_map, latent_grad
):
    n_gx, n_gy = lax.axis_size("gx"), lax.axis_size("gy")
    nz = ring_z(n_gx)
    ny = n_gx // nz
    cube, faces, down_rows, table = call(
        pack_kernel, "pack", [SM, SM, VM, VM], [VM] * 4,
        [shape(4, 64, 1024), shape(6, 4, 64, 128), shape(512, 128), shape(8, 128, dtype=jnp.int32)],
    )(counts, coarse_map, features, down_weight)
    remote, tables = call(
        bind(faces_kernel, n_gx, n_gy), "faces", [ANY, ANY], [ANY, ANY],
        [shape(4, 4, 64, 128), shape(3, 8, 128, dtype=jnp.int32)], [DMA((7,)), DMA((7,))], 0,
    )(faces, table)
    taps, hidden, act, octants = call(
        bind(level_kernel, n_gx, n_gy), "level", [SM] + [VM] * 5, [VM] * 4,
        [shape(4, 448, 1024), shape(4, 64, 1024, dtype=F32), shape(4, 512, 128), shape(8, 64, 128)],
        [pltpu.VMEM((6, 2, 9, 64, 128), BF16)],
    )(neighbours, cube, faces, remote, conv_weight, down_rows)
    received = call(
        merge_kernel, "merge_octants", [ANY], ANY, shape(24, 64, 128), [DMA((3,)), DMA((3,))], 1,
    )(octants)
    latent, coarse_grad, head_sum = call(
        coarse_kernel, "coarse", [SM] + [VM] * 4, [VM] * 3,
        [shape(1, 512, 128), shape(8, 64, 128), shape(128, 128)], [pltpu.VMEM((512, 128), BF16)],
    )(coarse_map, octants, received, head_weight, latent_grad)
    grad_received = call(
        merge_kernel, "merge_grads", [ANY], ANY, shape(24, 64, 128), [DMA((3,)), DMA((3,))], 2,
    )(coarse_grad)
    grads, hidden_grad, near_faces, far_faces = call(
        bind(backward_kernel, n_gx, n_gy), "backward", [SM] * 3 + [VM] * 7, [VM] * 4,
        [shape(GRAD_ROWS, 128), shape(4, 64, 1024), shape(6, 4, 64, 128, dtype=F32), shape(4, 4, 64, 128)],
        [
            pltpu.SMEM((8,), jnp.int32), pltpu.VMEM((6, 9, 64, 128), F32),
            pltpu.VMEM((64, 448), F32), pltpu.VMEM((512, 128), F32),
        ],
    )(
        neighbours, coarse_map, tables, coarse_grad, grad_received, hidden, act, taps, down_rows,
        head_sum,
    )
    far_in = call(
        bind(return_kernel, n_gx, n_gy), "return_faces", [ANY], ANY, shape(4, 4, 64, 128),
        [DMA((4,)), DMA((4,))], 3,
    )(far_faces)
    features_grad = call(
        final_kernel, "final", [SM] + [VM] * 4, VM, shape(8, 64, 512),
        [pltpu.VMEM((64, 448), BF16), pltpu.VMEM((448, 1024), BF16)],
    )(counts, conv_weight, hidden_grad, near_faces, far_in)
    per = GRAD_ROWS // (n_gy * nz)
    conv_grad, down_grad, head_grad = call(
        bind(sum_kernel, n_gx, n_gy), "sum_grads", [VM], [VM] * 3,
        [shape(64, 448, dtype=F32), shape(128, 512, dtype=F32), shape(128, 128, dtype=F32)],
        [
            pltpu.VMEM((n_gy, nz, per, 128), BF16), pltpu.VMEM((nz, per, 128), BF16),
            pltpu.VMEM((nz, per, 128), BF16), pltpu.VMEM((per, 128), F32),
            pltpu.VMEM((ny, per, 128), F32), pltpu.VMEM((nz, per, 128), BF16),
            pltpu.VMEM((n_gy, nz, per, 128), BF16),
            DMA((n_gy,)), DMA((n_gy,)), DMA((nz,)), DMA((nz,)), DMA((ny,)), DMA((ny,)),
            DMA((nz,)), DMA((nz,)), DMA((n_gy,)), DMA((n_gy,)),
        ],
        4,
    )(grads.reshape(n_gy, nz, per, 128))
    return (latent, features_grad, conv_grad, down_grad, head_grad)


def solution(mesh):
    placed = (
        P(("gx", "gy"), None, None),
        P(("gx", "gy"), None),
        P(("gx", "gy")),
        P(),
        P(),
        P(),
        P(("gx", "gy"), None),
        P(("gx", "gy"), None, None),
    )
    return jax.shard_map(
        body,
        mesh=mesh,
        in_specs=placed,
        out_specs=(P(("gx", "gy"), None, None), P(("gx", "gy"), None, None), P(), P(), P()),
        check_vma=False,
    )
```

```python
import jax
import jax.numpy as jnp
from jax import lax
from jax.experimental import pallas as pl
from jax.experimental.pallas import tpu as pltpu
from jax.sharding import PartitionSpec as P

MESH = pl.DeviceIdType.MESH
F32 = jnp.float32
BF16 = jnp.bfloat16
STRIDE = (16, 4, 1)
GRAD_ROWS = 1024


def ring_z(n_gx):
    return 8 if n_gx % 8 == 0 else n_gx // 2


def dot(a, b, ca, cb):
    return lax.dot_general(a, b, (((ca,), (cb,)), ((), ())), preferred_element_type=F32)


def lanes():
    return lax.broadcasted_iota(jnp.int32, (64, 128), 1)


def flag(value):
    return jnp.broadcast_to(value, (64, 128))


def roll(values, amount):
    amount = amount % 128
    return values if amount == 0 else pltpu.roll(values, amount, 1)


def column(axis, bit, s):
    high, low = s // 2, s % 2
    bits = [high, low]
    bits.insert(axis, bit)
    return bits[0] * 4 + bits[1] * 2 + bits[2]


def field(axis):
    return lax.rem(lax.div(lanes(), STRIDE[axis]), 4)


def pack_face(cols, axis, upper):
    step = STRIDE[axis]
    place = field(axis)
    out = None
    for s in range(4):
        shift = step * (s - 3) if upper else step * s
        moved = roll(cols[column(axis, int(upper), s)], shift)
        out = moved if out is None else jnp.where(place == s, moved, out)
    return out


def shift_minus(cols, axis, face):
    step = STRIDE[axis]
    edge = field(axis) == 0
    out = [None] * 8
    for s in range(4):
        low, high = column(axis, 0, s), column(axis, 1, s)
        out[high] = cols[low]
        out[low] = jnp.where(edge, roll(face, -step * s), roll(cols[high], step))
    return out


def shift_plus(cols, axis, face):
    step = STRIDE[axis]
    edge = field(axis) == 3
    out = [None] * 8
    for s in range(4):
        low, high = column(axis, 0, s), column(axis, 1, s)
        out[low] = cols[high]
        out[high] = jnp.where(edge, roll(face, step * (3 - s)), roll(cols[low], -step))
    return out


def sigmoid(values):
    return 1.0 / (1.0 + jnp.exp(-values))


def silu_grad(values):
    s = sigmoid(values)
    return s * (1.0 + values * (1.0 - s))


def edges(n_gx, n_gy):
    x, y = lax.axis_index("gx"), lax.axis_index("gy")
    return (x == 0, x == n_gx - 1, y == 0, y == n_gy - 1)


def link_of(links, slot, direction, rim):
    value = links[slot, direction]
    if direction < 4:
        return jnp.where(jnp.logical_and(rim[direction], value >= 8), 16, value)
    return value


def selection():
    row = lax.broadcasted_iota(jnp.int32, (512, 512), 0)
    col = lax.broadcasted_iota(jnp.int32, (512, 512), 1)
    return jnp.where(col == lax.rem(row, 64) * 8 + lax.div(row, 64), 1.0, 0.0).astype(BF16)


def around(n_gx, n_gy):
    x, y = lax.axis_index("gx"), lax.axis_index("gy")
    return (
        (lax.rem(x + 1, n_gx), y),
        (lax.rem(x + n_gx - 1, n_gx), y),
        (x, lax.rem(y + 1, n_gy)),
        (x, lax.rem(y + n_gy - 1, n_gy)),
    )


def partners():
    x, y = lax.axis_index("gx"), lax.axis_index("gy")
    x1 = x + 1 - 2 * lax.rem(x, 2)
    y1 = y + 1 - 2 * lax.rem(y, 2)
    return ((x1, y), (x, y1), (x1, y1))


def step_kernel(
    n_gx, n_gy, counts, links, maps, features, conv, down, head, grad_in,
    latent, out, total,
    faces, far, table, tables, down_rows, turned, pool, taps, hidden, act, octants, received,
    coarse_act, coarse_grad, grad_received, inverse, hidden_grad, planes, near, far_out, far_in,
    conv_acc, down_acc, final_taps, grads, part_a, sum_a, part_b, sum_b, part_c, part_d, part_e,
    face_s, face_r, merge_s, merge_r, back_s, back_r, ret_s, ret_r,
    send_a, recv_a, send_b, recv_b, send_c, recv_c, send_d, recv_d, send_e, recv_e,
):
    nz = ring_z(n_gx)
    ny = n_gx // nz
    x, me = lax.axis_index("gx"), lax.axis_index("gy")
    y, z = lax.div(x, nz), lax.rem(x, nz)
    beside = around(n_gx, n_gy)
    merged = partners()
    rows_g = [(x, lax.rem(me + k, n_gy)) for k in range(1, n_gy)]
    rows_z = [(y * nz + lax.rem(z + k, nz), me) for k in range(1, nz)]
    rows_y = [(lax.rem(y + k, ny) * nz + z, me) for k in range(1, ny)]
    everyone = list(beside) + list(merged) + rows_g + rows_z + rows_y
    rim = edges(n_gx, n_gy)
    low_half = lanes() < 64
    zero = jnp.zeros((64, 128), BF16)

    def send(source, target, sends, recvs, k, device):
        return pltpu.make_async_remote_copy(
            src_ref=source, dst_ref=target, send_sem=sends.at[k], recv_sem=recvs.at[k],
            device_id=device, device_id_type=MESH,
        )

    barrier = pltpu.get_barrier_semaphore()
    for device in everyone:
        pl.semaphore_signal(barrier, inc=1, device_id=device, device_id_type=MESH)

    def pack(i, carry):
        keep_a = flag(counts[0] - 2 * i) > 0
        keep_b = flag(counts[0] - 2 * i) > 1
        cols = [None] * 8
        for pq in range(4):
            a = jnp.where(keep_a, features[2 * i, :, pq * 128 : pq * 128 + 128], zero)
            b = jnp.where(keep_b, features[2 * i + 1, :, pq * 128 : pq * 128 + 128], zero)
            cols[2 * pq] = jnp.where(low_half, a, roll(b, 64))
            cols[2 * pq + 1] = jnp.where(low_half, roll(a, 64), b)
        for d in range(6):
            faces[d, i] = pack_face(cols, d // 2, d % 2 == 0)
        for c in range(8):
            taps[i, 0:64, c * 128 : c * 128 + 128] = cols[c]
        return carry

    lane = lax.broadcasted_iota(jnp.int32, (8, 128), 1)
    values = jnp.full((8, 128), -1, jnp.int32)
    for k in range(8):
        values = jnp.where(lane == k, jnp.broadcast_to(maps[0, k], (8, 128)), values)
    table[...] = values
    lax.fori_loop(0, 4, pack, 0)
    down_rows[...] = dot(selection(), down[...], 1, 1).astype(BF16)
    pl.semaphore_wait(barrier, len(everyone))
    face_copies = [
        send(faces.at[d], far.at[d], face_s, face_r, d, beside[d]) for d in range(4)
    ] + [send(table, tables.at[m], face_s, face_r, 4 + m, merged[m]) for m in range(3)]
    for copy in face_copies:
        copy.start()
    for d in range(6):
        pool[d, 0, 8] = zero
        pool[d, 1, 8] = zero

    def fill(j, carry):
        for d in range(6):
            own = faces[d, j]
            pool[d, 0, j] = own
            pool[d, 1, j] = roll(own, 64)
            if d >= 4:
                pool[d, 0, 4 + j] = zero
                pool[d, 1, 4 + j] = zero
        return carry

    lax.fori_loop(0, 4, fill, 0)

    def tap(i, d):
        cols = [taps[i, 0:64, c * 128 : c * 128 + 128] for c in range(8)]
        e0 = link_of(links, 2 * i, d, rim)
        e1 = link_of(links, 2 * i + 1, d, rim)
        face = jnp.where(
            low_half,
            pool[d, lax.rem(e0, 2), lax.div(e0, 2)],
            pool[d, 1 - lax.rem(e1, 2), lax.div(e1, 2)],
        )
        moved = (shift_minus if d % 2 == 0 else shift_plus)(cols, d // 2, face)
        for c in range(8):
            taps[i, 64 * (d + 1) : 64 * (d + 2), c * 128 : c * 128 + 128] = moved[c]

    def upright(i, carry):
        tap(i, 4)
        tap(i, 5)
        return carry

    lax.fori_loop(0, 4, upright, 0)
    for d in range(7):
        block = conv[:, d * 64 : d * 64 + 64].astype(F32)
        turned[:, d * 64 : d * 64 + 64] = block.T.astype(BF16)
    for copy in face_copies:
        copy.wait()

    def fill_far(j, carry):
        for d in range(4):
            pool[d, 0, 4 + j] = far[d, j]
            pool[d, 1, 4 + j] = roll(far[d, j], 64)
        return carry

    lax.fori_loop(0, 4, fill_far, 0)

    def chunk(source, target, sends, recvs, i, leg):
        rows = (source if leg < 2 else target).at[pl.ds(2 * i, 2)]
        place = target.at[pl.ds(8 * leg + 2 * i, 2)]
        return send(rows, place, sends, recvs, 4 * leg + i, merged[0] if leg == 0 else merged[1])

    def level(i, carry):
        for d in range(4):
            tap(i, d)
        values = dot(conv[...], taps[i], 1, 0)
        hidden[i] = values
        active = (values * sigmoid(values)).astype(BF16)
        for c in range(8):
            act[i, c * 64 : c * 64 + 64, :] = active[:, c * 128 : c * 128 + 128]
        rows = dot(act[i], down_rows[...], 0, 0).astype(BF16)
        octants[2 * i] = rows[:64]
        octants[2 * i + 1] = rows[64:]
        chunk(octants, received, merge_s, merge_r, i, 0).start()
        chunk(octants, received, merge_s, merge_r, i, 1).start()
        return carry

    lax.fori_loop(0, 4, level, 0)

    def relay(source, target, sends, recvs):
        def one(i, carry):
            chunk(source, target, sends, recvs, i, 0).wait_recv()
            chunk(source, target, sends, recvs, i, 2).start()
            return carry

        def rest(i, carry):
            chunk(source, target, sends, recvs, i, 0).wait_send()
            chunk(source, target, sends, recvs, i, 1).wait()
            chunk(source, target, sends, recvs, i, 2).wait()
            return carry

        lax.fori_loop(0, 4, one, 0)
        lax.fori_loop(0, 4, rest, 0)

    relay(octants, received, merge_s, merge_r)

    def merged_row(e, own, other):
        mine = own[jnp.clip(e, 0, 7)]
        theirs = other[jnp.clip(e - 8, 0, 23)]
        return jnp.where(flag(e) < 8, mine, jnp.where(flag(e) < 32, theirs, zero))

    def coarse(c, carry):
        values = jnp.concatenate([
            merged_row(maps[0, 2 * c], octants, received),
            merged_row(maps[0, 2 * c + 1], octants, received),
        ], axis=0).astype(F32)
        s = sigmoid(values)
        coarse_act[c] = (values * s).astype(BF16)
        back = dot(grad_in[c], head[...], 1, 0) * (s * (1.0 + values * (1.0 - s)))
        back = back.astype(BF16)
        coarse_grad[2 * c] = back[:64]
        coarse_grad[2 * c + 1] = back[64:]
        chunk(coarse_grad, grad_received, back_s, back_r, c, 0).start()
        chunk(coarse_grad, grad_received, back_s, back_r, c, 1).start()
        return carry

    lax.fori_loop(0, 4, coarse, 0)
    active = coarse_act[...].reshape(512, 128)
    latent[...] = dot(active, head[...], 1, 1).astype(BF16)
    grads[6] = dot(grad_in[...].reshape(512, 128), active, 0, 0).astype(BF16)
    grads[7] = jnp.zeros((128, 128), BF16)
    for s in range(8):
        found = jnp.zeros((8, 128), jnp.int32)
        for m in range(4):
            entries = table[...] if m == 0 else tables[m - 1]
            found = jnp.where(entries == m * 8 + s, m * 8 + lane - 32, found)
        inverse[s] = jnp.clip(jnp.sum(found[0:1, :]) + 32, 0, 32)
    conv_acc[...] = jnp.zeros_like(conv_acc)
    down_acc[...] = jnp.zeros_like(down_acc)
    relay(coarse_grad, grad_received, back_s, back_r)

    def backward(i, carry):
        rows = jnp.concatenate([
            merged_row(inverse[2 * i], coarse_grad, grad_received),
            merged_row(inverse[2 * i + 1], coarse_grad, grad_received),
        ], axis=0)
        down_acc[...] += dot(act[i], rows, 1, 0)
        patch = dot(down_rows[...], rows, 1, 1)
        for c in range(8):
            slope = silu_grad(hidden[i, :, c * 128 : c * 128 + 128])
            value = (patch[c * 64 : c * 64 + 64] * slope).astype(BF16)
            hidden_grad[i, :, c * 128 : c * 128 + 128] = value
        conv_acc[...] += dot(hidden_grad[i], taps[i], 1, 1)
        return carry

    lax.fori_loop(0, 4, backward, 0)
    wide = conv_acc[...].astype(BF16)
    grads[0, 0:64, :] = wide[:, 0:128]
    grads[0, 64:128, :] = wide[:, 128:256]
    grads[1, 0:64, :] = wide[:, 256:384]
    grads[1, 64:128, :] = jnp.concatenate([wide[:, 384:448], jnp.zeros((64, 64), BF16)], axis=1)
    ordered = dot(down_acc[...].astype(BF16), selection(), 0, 0).astype(BF16)
    for j in range(4):
        grads[2 + j] = ordered[:, j * 128 : j * 128 + 128]
    copies_a = [
        send(grads.at[lax.rem(me + k, n_gy)], part_a.at[k], send_a, recv_a, k, rows_g[k - 1])
        for k in range(1, n_gy)
    ]
    for copy in copies_a:
        copy.start()

    def plane(i, carry):
        cols = [hidden_grad[i, :, c * 128 : c * 128 + 128] for c in range(8)]
        for d in range(6):
            face = pack_face(cols, d // 2, d % 2 == 1)
            planes[d, 0, i] = face.astype(F32)
            planes[d, 1, i] = roll(face, 64).astype(F32)
        return carry

    lax.fori_loop(0, 4, plane, 0)

    def gathered(d, j):
        out = jnp.zeros((64, 128), F32)
        for i in range(4):
            e0 = link_of(links, 2 * i, d, rim)
            e1 = link_of(links, 2 * i + 1, d, rim)
            straight = jnp.where(low_half, flag(e0), flag(e1 - 1))
            crossed = jnp.where(low_half, flag(e1), flag(e0 - 1))
            out = out + jnp.where(straight == 2 * j, planes[d, 0, i], 0.0)
            out = out + jnp.where(crossed == 2 * j, planes[d, 1, i], 0.0)
        return out

    def collect_far(j, carry):
        for d in range(4):
            far_out[d, j] = gathered(d, 4 + j).astype(BF16)
        return carry

    def collect_near(j, carry):
        for d in range(6):
            near[d, j] = gathered(d, j)
        return carry

    lax.fori_loop(0, 4, collect_far, 0)
    target = (beside[1], beside[0], beside[3], beside[2])
    returns = [send(far_out.at[d], far_in.at[d], ret_s, ret_r, d, target[d]) for d in range(4)]
    for copy in returns:
        copy.start()
    for copy in copies_a:
        copy.wait()
    result = grads[me].astype(F32)
    for k in range(1, n_gy):
        result = result + part_a[k].astype(F32)
    per = result.shape[0] // nz
    result = result.reshape(nz, per, 128)
    sum_a[...] = result.astype(BF16)
    copies_b = [
        send(sum_a.at[lax.rem(z + k, nz)], part_b.at[k], send_b, recv_b, k, rows_z[k - 1])
        for k in range(1, nz)
    ]
    for copy in copies_b:
        copy.start()
    lax.fori_loop(0, 4, collect_near, 0)
    for copy in copies_b:
        copy.wait()
    result = sum_a[z].astype(F32)
    for k in range(1, nz):
        result = result + part_b[k].astype(F32)
    sum_b[...] = result
    part_c[y] = result
    copies_c = [
        send(sum_b, part_c.at[y], send_c, recv_c, k, rows_y[k - 1]) for k in range(1, ny)
    ]
    for copy in copies_c:
        copy.start()
    for copy in returns:
        copy.wait()

    def final(i, carry):
        cols = [hidden_grad[i, :, c * 128 : c * 128 + 128] for c in range(8)]
        for c in range(8):
            final_taps[0:64, c * 128 : c * 128 + 128] = cols[c]
        for d in range(6):
            face = near[d, i]
            if d < 4:
                face = face + far_in[d, i].astype(F32)
            moved = (shift_plus if d % 2 == 0 else shift_minus)(cols, d // 2, face.astype(BF16))
            for c in range(8):
                final_taps[64 * (d + 1) : 64 * (d + 2), c * 128 : c * 128 + 128] = moved[c]
        values = dot(turned[...], final_taps[...], 1, 0)
        keep_a = flag(counts[0] - 2 * i) > 0
        keep_b = flag(counts[0] - 2 * i) > 1
        for pq in range(4):
            even = values[:, pq * 256 : pq * 256 + 128]
            odd = values[:, pq * 256 + 128 : pq * 256 + 256]
            a = jnp.where(low_half, even, roll(odd, 64))
            b = jnp.where(low_half, roll(even, 64), odd)
            out[2 * i, :, pq * 128 : pq * 128 + 128] = jnp.where(keep_a, a, 0.0).astype(BF16)
            out[2 * i + 1, :, pq * 128 : pq * 128 + 128] = jnp.where(keep_b, b, 0.0).astype(BF16)
        return carry

    lax.fori_loop(0, 2, final, 0)
    for copy in copies_c:
        copy.wait()
    result = part_c[0]
    for k in range(1, ny):
        result = result + part_c[k]
    part_d[z] = result.astype(BF16)
    copies_d = [
        send(part_d.at[z], part_d.at[z], send_d, recv_d, k, rows_z[k - 1]) for k in range(1, nz)
    ]
    for copy in copies_d:
        copy.start()
    lax.fori_loop(2, 4, final, 0)
    for copy in copies_d:
        copy.wait()
    part_e[me] = part_d[...]
    copies_e = [
        send(part_d, part_e.at[me], send_e, recv_e, k, rows_g[k - 1]) for k in range(1, n_gy)
    ]
    for copy in copies_e:
        copy.start()
    for copy in copies_e:
        copy.wait()
    total[...] = part_e[...].reshape(n_gy, nz * per, 128)


def unpack_kernel(latent, features, total, latent_out, features_out, conv_out, down_out, head_out):
    scale = float(2048) ** -0.5
    latent_out[0] = latent[...]
    features_out[...] = features[...]
    rows = total[...].reshape(GRAD_ROWS, 128).astype(F32) * scale
    for j in range(3):
        conv_out[:, j * 128 : j * 128 + 128] = rows[j * 64 : j * 64 + 64]
    conv_out[:, 384:448] = rows[192:256, :64]
    for j in range(4):
        down_out[:, j * 128 : j * 128 + 128] = rows[256 + j * 128 : 384 + j * 128]
    head_out[...] = rows[768:896]


VM = pl.BlockSpec(memory_space=pltpu.VMEM)
SM = pl.BlockSpec(memory_space=pltpu.SMEM)
DMA = pltpu.SemaphoreType.DMA
VMEM = pltpu.VMEM


def shape(*dims, dtype=BF16):
    return jax.ShapeDtypeStruct(dims, dtype)


def bind(kernel, *fixed):
    def run(*refs):
        kernel(*fixed, *refs)

    return run


def body(
    features, neighbours, counts, conv_weight, down_weight, head_weight, coarse_map, latent_grad
):
    n_gx, n_gy = lax.axis_size("gx"), lax.axis_size("gy")
    nz = ring_z(n_gx)
    ny = n_gx // nz
    part = GRAD_ROWS // n_gy
    per = part // nz
    latent, grad, total = pl.pallas_call(
        bind(step_kernel, n_gx, n_gy), name="step", in_specs=[SM] * 3 + [VM] * 5,
        out_specs=[VM] * 3,
        out_shape=[shape(512, 128), shape(8, 64, 512), shape(n_gy, part, 128)],
        scratch_shapes=[
            VMEM((6, 4, 64, 128), BF16), VMEM((4, 4, 64, 128), BF16),
            VMEM((8, 128), jnp.int32), VMEM((3, 8, 128), jnp.int32),
            VMEM((512, 128), BF16), VMEM((64, 448), BF16), VMEM((6, 2, 9, 64, 128), BF16),
            VMEM((4, 448, 1024), BF16), VMEM((4, 64, 1024), F32), VMEM((4, 512, 128), BF16),
            VMEM((8, 64, 128), BF16), VMEM((24, 64, 128), BF16),
            VMEM((4, 128, 128), BF16), VMEM((8, 64, 128), BF16), VMEM((24, 64, 128), BF16),
            pltpu.SMEM((8,), jnp.int32), VMEM((4, 64, 1024), BF16), VMEM((6, 2, 4, 64, 128), F32),
            VMEM((6, 4, 64, 128), F32), VMEM((4, 4, 64, 128), BF16), VMEM((4, 4, 64, 128), BF16),
            VMEM((64, 448), F32), VMEM((512, 128), F32), VMEM((448, 1024), BF16),
            VMEM((n_gy, part, 128), BF16), VMEM((n_gy, part, 128), BF16),
            VMEM((nz, per, 128), BF16), VMEM((nz, per, 128), BF16), VMEM((per, 128), F32),
            VMEM((ny, per, 128), F32), VMEM((nz, per, 128), BF16),
            VMEM((n_gy, nz, per, 128), BF16),
            DMA((7,)), DMA((7,)), DMA((12,)), DMA((12,)), DMA((12,)), DMA((12,)),
            DMA((4,)), DMA((4,)),
            DMA((n_gy,)), DMA((n_gy,)), DMA((nz,)), DMA((nz,)), DMA((ny,)), DMA((ny,)),
            DMA((nz,)), DMA((nz,)), DMA((n_gy,)), DMA((n_gy,)),
        ],
        compiler_params=pltpu.CompilerParams(collective_id=0, has_side_effects=True),
    )(
        counts, neighbours, coarse_map, features, conv_weight, down_weight, head_weight,
        latent_grad.reshape(4, 128, 128),
    )
    return pl.pallas_call(
        unpack_kernel, name="unpack", in_specs=[VM] * 3, out_specs=[VM] * 5,
        out_shape=[
            shape(1, 512, 128), shape(8, 64, 512), shape(64, 448, dtype=F32),
            shape(128, 512, dtype=F32), shape(128, 128, dtype=F32),
        ],
    )(latent, grad, total)


def solution(mesh):
    placed = (
        P(("gx", "gy"), None, None),
        P(("gx", "gy"), None),
        P(("gx", "gy")),
        P(),
        P(),
        P(),
        P(("gx", "gy"), None),
        P(("gx", "gy"), None, None),
    )
    return jax.shard_map(
        body,
        mesh=mesh,
        in_specs=placed,
        out_specs=(P(("gx", "gy"), None, None), P(("gx", "gy"), None, None), P(), P(), P()),
        check_vma=False,
    )
```

```python
import jax
import jax.numpy as jnp
from jax import lax
from jax.experimental import pallas as pl
from jax.experimental.pallas import tpu as pltpu
from jax.sharding import PartitionSpec as P

MESH = pl.DeviceIdType.MESH
F32 = jnp.float32
BF16 = jnp.bfloat16
STRIDE = (16, 4, 1)
GRAD_ROWS = 1024


def ring_z(n_gx):
    return 8 if n_gx % 8 == 0 else n_gx // 2


def dot(a, b, ca, cb):
    return lax.dot_general(a, b, (((ca,), (cb,)), ((), ())), preferred_element_type=F32)


def lanes():
    return lax.broadcasted_iota(jnp.int32, (64, 128), 1)


def flag(value):
    return jnp.broadcast_to(value, (64, 128))


def roll(values, amount):
    amount = amount % 128
    return values if amount == 0 else pltpu.roll(values, amount, 1)


def column(axis, bit, s):
    high, low = s // 2, s % 2
    bits = [high, low]
    bits.insert(axis, bit)
    return bits[0] * 4 + bits[1] * 2 + bits[2]


def field(axis):
    return lax.rem(lax.div(lanes(), STRIDE[axis]), 4)


def pack_face(cols, axis, upper):
    step = STRIDE[axis]
    place = field(axis)
    out = None
    for s in range(4):
        shift = step * (s - 3) if upper else step * s
        moved = roll(cols[column(axis, int(upper), s)], shift)
        out = moved if out is None else jnp.where(place == s, moved, out)
    return out


def shift_minus(cols, axis, face):
    step = STRIDE[axis]
    edge = field(axis) == 0
    out = [None] * 8
    for s in range(4):
        low, high = column(axis, 0, s), column(axis, 1, s)
        out[high] = cols[low]
        out[low] = jnp.where(edge, roll(face, -step * s), roll(cols[high], step))
    return out


def shift_plus(cols, axis, face):
    step = STRIDE[axis]
    edge = field(axis) == 3
    out = [None] * 8
    for s in range(4):
        low, high = column(axis, 0, s), column(axis, 1, s)
        out[low] = cols[high]
        out[high] = jnp.where(edge, roll(face, step * (3 - s)), roll(cols[low], -step))
    return out


def sigmoid(values):
    return 1.0 / (1.0 + jnp.exp(-values))


def silu_grad(values):
    s = sigmoid(values)
    return s * (1.0 + values * (1.0 - s))


def edges(n_gx, n_gy):
    x, y = lax.axis_index("gx"), lax.axis_index("gy")
    return (x == 0, x == n_gx - 1, y == 0, y == n_gy - 1)


def link_of(links, slot, direction, rim):
    value = links[slot, direction]
    if direction < 4:
        return jnp.where(jnp.logical_and(rim[direction], value >= 8), 16, value)
    return value


def selection():
    row = lax.broadcasted_iota(jnp.int32, (512, 512), 0)
    col = lax.broadcasted_iota(jnp.int32, (512, 512), 1)
    return jnp.where(col == lax.rem(row, 64) * 8 + lax.div(row, 64), 1.0, 0.0).astype(BF16)


def around(n_gx, n_gy):
    x, y = lax.axis_index("gx"), lax.axis_index("gy")
    return (
        (lax.rem(x + 1, n_gx), y),
        (lax.rem(x + n_gx - 1, n_gx), y),
        (x, lax.rem(y + 1, n_gy)),
        (x, lax.rem(y + n_gy - 1, n_gy)),
    )


def partners():
    x, y = lax.axis_index("gx"), lax.axis_index("gy")
    x1 = x + 1 - 2 * lax.rem(x, 2)
    y1 = y + 1 - 2 * lax.rem(y, 2)
    return ((x1, y), (x, y1), (x1, y1))


def step_kernel(
    n_gx, n_gy, counts, links, maps, conv, down, head, features, grad_in,
    latent, out, total,
    blocks, grad_own, grad_far, faces, far, table, tables, down_rows, turned, pool, taps, hidden,
    act, octants, received, inverse, hidden_grad, planes, near, far_out, far_in, conv_acc, down_acc,
    head_acc, final_taps, coarse, latent_own, out_own,
    grads, part_0, sum_0, part_1, part_2, part_3,
    load_s, store_s, face_s, face_r, merge_s, merge_r, back_s, back_r, ret_s, ret_r,
    send_0, recv_0, send_1, recv_1, send_2, recv_2, send_3, recv_3, send_4, recv_4,
):
    nz = ring_z(n_gx)
    ny, nc = n_gx // nz, n_gy // 2
    plane_size = nc * ny
    x, me = lax.axis_index("gx"), lax.axis_index("gy")
    y, z = lax.div(x, nz), lax.rem(x, nz)
    chip, core = lax.div(me, 2), lax.rem(me, 2)
    spot = chip * ny + y
    beside = around(n_gx, n_gy)
    merged = partners()
    mate = merged[1]
    rows_z = [(y * nz + lax.rem(z + k, nz), me) for k in range(1, nz)]
    rows_p, spots = [None], [None]
    for k in range(1, plane_size):
        other_c = lax.rem(chip + k // ny, nc)
        other_y = lax.rem(y + k % ny, ny)
        rows_p.append((other_y * nz + z, other_c * 2 + core))
        spots.append(other_c * ny + other_y)
    everyone = list(beside) + list(merged) + rows_z + rows_p[1:]
    rim = edges(n_gx, n_gy)
    low_half = lanes() < 64
    zero = jnp.zeros((64, 128), BF16)

    def send(source, target, sends, recvs, k, device):
        return pltpu.make_async_remote_copy(
            src_ref=source, dst_ref=target, send_sem=sends.at[k], recv_sem=recvs.at[k],
            device_id=device, device_id_type=MESH,
        )

    barrier = pltpu.get_barrier_semaphore()
    for device in everyone:
        pl.semaphore_signal(barrier, inc=1, device_id=device, device_id_type=MESH)

    def load(i):
        return pltpu.make_async_copy(
            features.at[pl.ds(2 * i, 2)], blocks.at[pl.ds(2 * i, 2)], load_s.at[i]
        )

    for i in range(4):
        load(i).start()
    grad_load = pltpu.make_async_copy(grad_in, grad_own, load_s.at[4])
    grad_load.start()
    lane = lax.broadcasted_iota(jnp.int32, (8, 128), 1)
    values = jnp.full((8, 128), -1, jnp.int32)
    for k in range(8):
        values = jnp.where(lane == k, jnp.broadcast_to(maps[0, k], (8, 128)), values)
    table[...] = values
    down_rows[...] = dot(selection(), down[...], 1, 1).astype(BF16)

    def pack(i, carry):
        load(i).wait()
        keep_a = flag(counts[0] - 2 * i) > 0
        keep_b = flag(counts[0] - 2 * i) > 1
        cols = [None] * 8
        for pq in range(4):
            a = jnp.where(keep_a, blocks[2 * i, :, pq * 128 : pq * 128 + 128], zero)
            b = jnp.where(keep_b, blocks[2 * i + 1, :, pq * 128 : pq * 128 + 128], zero)
            cols[2 * pq] = jnp.where(low_half, a, roll(b, 64))
            cols[2 * pq + 1] = jnp.where(low_half, roll(a, 64), b)
        for d in range(6):
            faces[d, i] = pack_face(cols, d // 2, d % 2 == 0)
        for c in range(8):
            taps[i, 0:64, c * 128 : c * 128 + 128] = cols[c]
        return carry

    lax.fori_loop(0, 4, pack, 0)
    grad_load.wait()
    pl.semaphore_wait(barrier, len(everyone))
    face_copies = [
        send(faces.at[d], far.at[d], face_s, face_r, d, beside[d]) for d in range(4)
    ] + [send(table, tables.at[m], face_s, face_r, 4 + m, merged[m]) for m in range(3)]
    for copy in face_copies:
        copy.start()

    def chunk(source, target, sends, recvs, i, leg):
        rows = (source if leg < 2 else target).at[pl.ds(2 * i, 2)]
        place = target.at[pl.ds(8 * leg + 2 * i, 2)]
        return send(rows, place, sends, recvs, 4 * leg + i, merged[0] if leg == 0 else mate)

    def grad_chunk(i, leg):
        return chunk(grad_own, grad_far, back_s, back_r, i, leg)

    def octant_chunk(i, leg):
        return chunk(octants, received, merge_s, merge_r, i, leg)

    for i in range(4):
        grad_chunk(i, 0).start()
        grad_chunk(i, 1).start()
    for d in range(6):
        pool[d, 0, 8] = zero
        pool[d, 1, 8] = zero

    def fill(j, carry):
        for d in range(6):
            own = faces[d, j]
            pool[d, 0, j] = own
            pool[d, 1, j] = roll(own, 64)
            if d >= 4:
                pool[d, 0, 4 + j] = zero
                pool[d, 1, 4 + j] = zero
        return carry

    lax.fori_loop(0, 4, fill, 0)

    def tap(i, d):
        cols = [taps[i, 0:64, c * 128 : c * 128 + 128] for c in range(8)]
        e0 = link_of(links, 2 * i, d, rim)
        e1 = link_of(links, 2 * i + 1, d, rim)
        face = jnp.where(
            low_half,
            pool[d, lax.rem(e0, 2), lax.div(e0, 2)],
            pool[d, 1 - lax.rem(e1, 2), lax.div(e1, 2)],
        )
        moved = (shift_minus if d % 2 == 0 else shift_plus)(cols, d // 2, face)
        for c in range(8):
            taps[i, 64 * (d + 1) : 64 * (d + 2), c * 128 : c * 128 + 128] = moved[c]

    def upright(i, carry):
        tap(i, 4)
        tap(i, 5)
        return carry

    lax.fori_loop(0, 4, upright, 0)
    for d in range(7):
        block = conv[:, d * 64 : d * 64 + 64].astype(F32)
        turned[:, d * 64 : d * 64 + 64] = block.T.astype(BF16)
    conv_acc[...] = jnp.zeros_like(conv_acc)
    down_acc[...] = jnp.zeros_like(down_acc)
    head_acc[...] = jnp.zeros_like(head_acc)
    for copy in face_copies:
        copy.wait()

    def fill_far(j, carry):
        for d in range(4):
            pool[d, 0, 4 + j] = far[d, j]
            pool[d, 1, 4 + j] = roll(far[d, j], 64)
        return carry

    lax.fori_loop(0, 4, fill_far, 0)

    def level(i, carry):
        for d in range(4):
            tap(i, d)
        values = dot(conv[...], taps[i], 1, 0)
        hidden[i] = values
        active = (values * sigmoid(values)).astype(BF16)
        for c in range(8):
            act[i, c * 64 : c * 64 + 64, :] = active[:, c * 128 : c * 128 + 128]
        rows = dot(act[i], down_rows[...], 0, 0).astype(BF16)
        octants[2 * i] = rows[:64]
        octants[2 * i + 1] = rows[64:]
        octant_chunk(i, 0).start()
        octant_chunk(i, 1).start()
        grad_chunk(i, 0).wait_recv()
        grad_chunk(i, 2).start()
        return carry

    lax.fori_loop(0, 4, level, 0)
    for s in range(8):
        found = jnp.zeros((8, 128), jnp.int32)
        for m in range(4):
            entries = table[...] if m == 0 else tables[m - 1]
            found = jnp.where(entries == m * 8 + s, m * 8 + lane - 32, found)
        inverse[s] = jnp.clip(jnp.sum(found[0:1, :]) + 32, 0, 32)

    def settle(part):
        def rest(i, carry):
            part(i, 0).wait_send()
            part(i, 1).wait()
            part(i, 2).wait()
            return carry

        lax.fori_loop(0, 4, rest, 0)

    settle(grad_chunk)

    def merged_row(e, own, other):
        mine = own[jnp.clip(e, 0, 7)]
        theirs = other[jnp.clip(e - 8, 0, 23)]
        return jnp.where(flag(e) < 8, mine, jnp.where(flag(e) < 32, theirs, zero))

    def backward(i, carry):
        named = jnp.concatenate([
            merged_row(inverse[2 * i], grad_own, grad_far),
            merged_row(inverse[2 * i + 1], grad_own, grad_far),
        ], axis=0)
        values = jnp.concatenate([octants[2 * i], octants[2 * i + 1]], axis=0).astype(F32)
        s = sigmoid(values)
        active = (values * s).astype(BF16)
        head_acc[...] += dot(named, active, 0, 0)
        rows = dot(named, head[...], 1, 0) * (s * (1.0 + values * (1.0 - s)))
        rows = rows.astype(BF16)
        down_acc[...] += dot(act[i], rows, 1, 0)
        patch = dot(down_rows[...], rows, 1, 1)
        for c in range(8):
            slope = silu_grad(hidden[i, :, c * 128 : c * 128 + 128])
            value = (patch[c * 64 : c * 64 + 64] * slope).astype(BF16)
            hidden_grad[i, :, c * 128 : c * 128 + 128] = value
        conv_acc[...] += dot(hidden_grad[i], taps[i], 1, 1)
        return carry

    lax.fori_loop(0, 4, backward, 0)
    wide = conv_acc[...].astype(BF16)
    for j in range(3):
        grads[0, j * 64 : j * 64 + 64, :] = wide[:, j * 128 : j * 128 + 128]
    grads[0, 192:256, :] = jnp.concatenate([wide[:, 384:448], jnp.zeros((64, 64), BF16)], axis=1)
    ordered = dot(down_acc[...].astype(BF16), selection(), 0, 0).astype(BF16)
    for j in range(4):
        row = 256 + 128 * (j % 2) if j < 2 else 128 * (j % 2)
        grads[j // 2, row : row + 128, :] = ordered[:, j * 128 : j * 128 + 128]
    grads[1, 256:384, :] = head_acc[...].astype(BF16)
    grads[1, 384:512, :] = jnp.zeros((128, 128), BF16)
    copy_0 = send(grads.at[1 - core], part_0, send_0, recv_0, 0, mate)
    copy_0.start()

    def relay(i, carry):
        octant_chunk(i, 0).wait_recv()
        octant_chunk(i, 2).start()
        return carry

    lax.fori_loop(0, 4, relay, 0)

    def plane(i, carry):
        cols = [hidden_grad[i, :, c * 128 : c * 128 + 128] for c in range(8)]
        for d in range(6):
            face = pack_face(cols, d // 2, d % 2 == 1)
            planes[d, 0, i] = face.astype(F32)
            planes[d, 1, i] = roll(face, 64).astype(F32)
        return carry

    def gathered(d, j):
        out = jnp.zeros((64, 128), F32)
        for i in range(4):
            e0 = link_of(links, 2 * i, d, rim)
            e1 = link_of(links, 2 * i + 1, d, rim)
            straight = jnp.where(low_half, flag(e0), flag(e1 - 1))
            crossed = jnp.where(low_half, flag(e1), flag(e0 - 1))
            out = out + jnp.where(straight == 2 * j, planes[d, 0, i], 0.0)
            out = out + jnp.where(crossed == 2 * j, planes[d, 1, i], 0.0)
        return out

    def collect_far(j, carry):
        for d in range(4):
            far_out[d, j] = gathered(d, 4 + j).astype(BF16)
        return carry

    def collect_near(j, carry):
        for d in range(6):
            near[d, j] = gathered(d, j)
        return carry

    copy_0.wait()
    result = grads[core].astype(F32) + part_0[...].astype(F32)
    per = result.shape[0] // plane_size
    sum_0[...] = result.astype(BF16).reshape(plane_size, per, 128)
    copies_1 = [
        send(sum_0.at[spots[k]], part_1.at[k], send_1, recv_1, k, rows_p[k])
        for k in range(1, plane_size)
    ]
    for copy in copies_1:
        copy.start()
    lax.fori_loop(0, 4, plane, 0)
    lax.fori_loop(0, 4, collect_far, 0)
    target = (beside[1], beside[0], beside[3], beside[2])
    returns = [send(far_out.at[d], far_in.at[d], ret_s, ret_r, d, target[d]) for d in range(4)]
    for copy in returns:
        copy.start()
    for copy in copies_1:
        copy.wait()
    result = sum_0[spot].astype(F32)
    for k in range(1, plane_size):
        result = result + part_1[k].astype(F32)
    part_2[z] = result.astype(BF16)
    copies_2 = [
        send(part_2.at[z], part_2.at[z], send_2, recv_2, k, rows_z[k - 1]) for k in range(1, nz)
    ]
    for copy in copies_2:
        copy.start()
    settle(octant_chunk)
    for k in range(8):
        coarse[k * 64 : k * 64 + 64, :] = merged_row(maps[0, k], octants, received)
    values = coarse[...].astype(F32)
    active = (values * sigmoid(values)).astype(BF16)
    latent_own[...] = dot(active, head[...], 1, 1).astype(BF16)
    lax.fori_loop(0, 4, collect_near, 0)
    for copy in returns:
        copy.wait()

    def store(i):
        return pltpu.make_async_copy(
            out_own.at[pl.ds(2 * i, 2)], out.at[pl.ds(2 * i, 2)], store_s.at[i]
        )

    def final(i, carry):
        cols = [hidden_grad[i, :, c * 128 : c * 128 + 128] for c in range(8)]
        for c in range(8):
            final_taps[0:64, c * 128 : c * 128 + 128] = cols[c]
        for d in range(6):
            face = near[d, i]
            if d < 4:
                face = face + far_in[d, i].astype(F32)
            moved = (shift_plus if d % 2 == 0 else shift_minus)(cols, d // 2, face.astype(BF16))
            for c in range(8):
                final_taps[64 * (d + 1) : 64 * (d + 2), c * 128 : c * 128 + 128] = moved[c]
        values = dot(turned[...], final_taps[...], 1, 0)
        keep_a = flag(counts[0] - 2 * i) > 0
        keep_b = flag(counts[0] - 2 * i) > 1
        for pq in range(4):
            even = values[:, pq * 256 : pq * 256 + 128]
            odd = values[:, pq * 256 + 128 : pq * 256 + 256]
            a = jnp.where(low_half, even, roll(odd, 64))
            b = jnp.where(low_half, roll(even, 64), odd)
            spread = slice(pq * 128, pq * 128 + 128)
            out_own[2 * i, :, spread] = jnp.where(keep_a, a, 0.0).astype(BF16)
            out_own[2 * i + 1, :, spread] = jnp.where(keep_b, b, 0.0).astype(BF16)
        return carry

    for copy in copies_2:
        copy.wait()
    result = part_2[0].astype(F32)
    for k in range(1, nz):
        result = result + part_2[k].astype(F32)
    part_3[spot] = result.astype(BF16)
    copies_3 = [
        send(part_3.at[spot], part_3.at[spot], send_3, recv_3, k, rows_p[k])
        for k in range(1, plane_size)
    ]
    for copy in copies_3:
        copy.start()
    lax.fori_loop(0, 4, final, 0)
    latent_store = pltpu.make_async_copy(latent_own, latent, store_s.at[4])
    latent_store.start()
    for i in range(4):
        store(i).start()
    for copy in copies_3:
        copy.wait()
    copy_4 = send(part_3, total.at[core], send_4, recv_4, 0, mate)
    copy_4.start()
    own_store = pltpu.make_async_copy(part_3, total.at[core], store_s.at[5])
    own_store.start()
    latent_store.wait()
    for i in range(4):
        store(i).wait()
    own_store.wait()
    copy_4.wait()


def unpack_kernel(
    latent, features, total, latent_out, features_out, conv_out, down_out, head_out,
    latent_hold, features_hold, total_hold, load_s, store_s,
):
    scale = float(2048) ** -0.5
    total_load = pltpu.make_async_copy(total, total_hold, load_s.at[0])
    latent_load = pltpu.make_async_copy(latent, latent_hold, load_s.at[1])
    features_load = pltpu.make_async_copy(features, features_hold, load_s.at[2])
    total_load.start()
    latent_load.start()
    features_load.start()
    latent_load.wait()
    latent_store = pltpu.make_async_copy(latent_hold, latent_out.at[0], store_s.at[0])
    latent_store.start()
    features_load.wait()
    features_store = pltpu.make_async_copy(features_hold, features_out, store_s.at[1])
    features_store.start()
    total_load.wait()
    rows = total_hold[...].reshape(GRAD_ROWS, 128).astype(F32) * scale
    for j in range(3):
        conv_out[:, j * 128 : j * 128 + 128] = rows[j * 64 : j * 64 + 64]
    conv_out[:, 384:448] = rows[192:256, :64]
    for j in range(4):
        down_out[:, j * 128 : j * 128 + 128] = rows[256 + j * 128 : 384 + j * 128]
    head_out[...] = rows[768:896]
    latent_store.wait()
    features_store.wait()


VM = pl.BlockSpec(memory_space=pltpu.VMEM)
SM = pl.BlockSpec(memory_space=pltpu.SMEM)
ANY = pl.BlockSpec(memory_space=pl.ANY)
DMA = pltpu.SemaphoreType.DMA
VMEM = pltpu.VMEM


def shape(*dims, dtype=BF16):
    return jax.ShapeDtypeStruct(dims, dtype)


def bind(kernel, *fixed):
    def run(*refs):
        kernel(*fixed, *refs)

    return run


def body(
    features, neighbours, counts, conv_weight, down_weight, head_weight, coarse_map, latent_grad
):
    n_gx, n_gy = lax.axis_size("gx"), lax.axis_size("gy")
    nz = ring_z(n_gx)
    spots = (n_gx // nz) * (n_gy // 2)
    per = GRAD_ROWS // 2 // spots
    pairs = [DMA((1,)), DMA((spots,)), DMA((nz,)), DMA((spots,)), DMA((1,))]
    latent, grad, total = pl.pallas_call(
        bind(step_kernel, n_gx, n_gy), name="step", in_specs=[SM] * 3 + [VM] * 3 + [ANY] * 2,
        out_specs=[ANY] * 3,
        out_shape=[shape(512, 128), shape(8, 64, 512), shape(2, spots, per, 128)],
        scratch_shapes=[
            VMEM((8, 64, 512), BF16), VMEM((8, 64, 128), BF16), VMEM((24, 64, 128), BF16),
            VMEM((6, 4, 64, 128), BF16), VMEM((4, 4, 64, 128), BF16),
            VMEM((8, 128), jnp.int32), VMEM((3, 8, 128), jnp.int32),
            VMEM((512, 128), BF16), VMEM((64, 448), BF16), VMEM((6, 2, 9, 64, 128), BF16),
            VMEM((4, 448, 1024), BF16), VMEM((4, 64, 1024), F32), VMEM((4, 512, 128), BF16),
            VMEM((8, 64, 128), BF16), VMEM((24, 64, 128), BF16),
            pltpu.SMEM((8,), jnp.int32), VMEM((4, 64, 1024), BF16), VMEM((6, 2, 4, 64, 128), F32),
            VMEM((6, 4, 64, 128), F32), VMEM((4, 4, 64, 128), BF16), VMEM((4, 4, 64, 128), BF16),
            VMEM((64, 448), F32), VMEM((512, 128), F32), VMEM((128, 128), F32),
            VMEM((448, 1024), BF16), VMEM((512, 128), BF16), VMEM((512, 128), BF16),
            VMEM((8, 64, 512), BF16),
            VMEM((2, 512, 128), BF16), VMEM((512, 128), BF16), VMEM((spots, per, 128), BF16),
            VMEM((spots, per, 128), BF16), VMEM((nz, per, 128), BF16), VMEM((spots, per, 128), BF16),
            DMA((5,)), DMA((6,)),
            DMA((7,)), DMA((7,)), DMA((12,)), DMA((12,)), DMA((12,)), DMA((12,)),
            DMA((4,)), DMA((4,)),
        ] + [pair for pair in pairs for _ in range(2)],
        compiler_params=pltpu.CompilerParams(collective_id=0, has_side_effects=True),
    )(
        counts, neighbours, coarse_map, conv_weight, down_weight, head_weight, features,
        latent_grad.reshape(8, 64, 128),
    )
    return pl.pallas_call(
        unpack_kernel, name="unpack", in_specs=[ANY] * 3, out_specs=[ANY] * 2 + [VM] * 3,
        out_shape=[
            shape(1, 512, 128), shape(8, 64, 512), shape(64, 448, dtype=F32),
            shape(128, 512, dtype=F32), shape(128, 128, dtype=F32),
        ],
        scratch_shapes=[
            VMEM((512, 128), BF16), VMEM((8, 64, 512), BF16), VMEM((2, spots, per, 128), BF16),
            DMA((3,)), DMA((2,)),
        ],
    )(latent, grad, total)


def solution(mesh):
    placed = (
        P(("gx", "gy"), None, None),
        P(("gx", "gy"), None),
        P(("gx", "gy")),
        P(),
        P(),
        P(),
        P(("gx", "gy"), None),
        P(("gx", "gy"), None, None),
    )
    return jax.shard_map(
        body,
        mesh=mesh,
        in_specs=placed,
        out_specs=(P(("gx", "gy"), None, None), P(("gx", "gy"), None, None), P(), P(), P()),
        check_vma=False,
    )
```

```python
import jax
import jax.numpy as jnp
from jax import lax
from jax.experimental import pallas as pl
from jax.experimental.pallas import tpu as pltpu
from jax.sharding import PartitionSpec as P

MESH = pl.DeviceIdType.MESH
F32 = jnp.float32
BF16 = jnp.bfloat16
STRIDE = (16, 4, 1)
GRAD_ROWS = 1024


def ring_z(n_gx):
    return 8 if n_gx % 8 == 0 else n_gx // 2


def dot(a, b, ca, cb):
    return lax.dot_general(a, b, (((ca,), (cb,)), ((), ())), preferred_element_type=F32)


def lanes():
    return lax.broadcasted_iota(jnp.int32, (64, 128), 1)


def flag(value):
    return jnp.broadcast_to(value, (64, 128))


def roll(values, amount):
    amount = amount % 128
    return values if amount == 0 else pltpu.roll(values, amount, 1)


def column(axis, bit, s):
    high, low = s // 2, s % 2
    bits = [high, low]
    bits.insert(axis, bit)
    return bits[0] * 4 + bits[1] * 2 + bits[2]


def field(axis):
    return lax.rem(lax.div(lanes(), STRIDE[axis]), 4)


def pack_face(cols, axis, upper):
    step = STRIDE[axis]
    place = field(axis)
    out = None
    for s in range(4):
        shift = step * (s - 3) if upper else step * s
        moved = roll(cols[column(axis, int(upper), s)], shift)
        out = moved if out is None else jnp.where(place == s, moved, out)
    return out


def shift_minus(cols, axis, face):
    step = STRIDE[axis]
    edge = field(axis) == 0
    out = [None] * 8
    for s in range(4):
        low, high = column(axis, 0, s), column(axis, 1, s)
        out[high] = cols[low]
        out[low] = jnp.where(edge, roll(face, -step * s), roll(cols[high], step))
    return out


def shift_plus(cols, axis, face):
    step = STRIDE[axis]
    edge = field(axis) == 3
    out = [None] * 8
    for s in range(4):
        low, high = column(axis, 0, s), column(axis, 1, s)
        out[low] = cols[high]
        out[high] = jnp.where(edge, roll(face, step * (3 - s)), roll(cols[low], -step))
    return out


def sigmoid(values):
    return 1.0 / (1.0 + jnp.exp(-values))


def silu_grad(values):
    s = sigmoid(values)
    return s * (1.0 + values * (1.0 - s))


def edges(n_gx, n_gy):
    x, y = lax.axis_index("gx"), lax.axis_index("gy")
    return (x == 0, x == n_gx - 1, y == 0, y == n_gy - 1)


def link_of(links, slot, direction, rim):
    value = links[slot, direction]
    if direction < 4:
        return jnp.where(jnp.logical_and(rim[direction], value >= 8), 16, value)
    return value


def selection():
    row = lax.broadcasted_iota(jnp.int32, (512, 512), 0)
    col = lax.broadcasted_iota(jnp.int32, (512, 512), 1)
    return jnp.where(col == lax.rem(row, 64) * 8 + lax.div(row, 64), 1.0, 0.0).astype(BF16)


def around(n_gx, n_gy):
    x, y = lax.axis_index("gx"), lax.axis_index("gy")
    return (
        (lax.rem(x + 1, n_gx), y),
        (lax.rem(x + n_gx - 1, n_gx), y),
        (x, lax.rem(y + 1, n_gy)),
        (x, lax.rem(y + n_gy - 1, n_gy)),
    )


def partners():
    x, y = lax.axis_index("gx"), lax.axis_index("gy")
    x1 = x + 1 - 2 * lax.rem(x, 2)
    y1 = y + 1 - 2 * lax.rem(y, 2)
    return ((x1, y), (x, y1), (x1, y1))


def step_kernel(
    n_gx, n_gy, counts, links, maps, conv_in, down_in, head_in, features, grad_in,
    latent, out, total,
    conv, down, head, blocks, grad_own, grad_far, table, tables, down_rows, turned, pool, tall, taps, hidden,
    act, octants, received, inverse, hidden_grad, planes, near, far_out, far_in, conv_acc, down_acc,
    head_acc, final_taps, coarse,
    grads, part_0, sum_0, part_1, part_2, part_3,
    load_s, face_s, face_r, merge_s, merge_r, back_s, back_r, ret_s, ret_r,
    send_0, recv_0, send_1, recv_1, send_2, recv_2, send_3, recv_3, send_4, recv_4,
):
    nz = ring_z(n_gx)
    ny, nc = n_gx // nz, n_gy // 2
    plane_size = nc * ny
    x, me = lax.axis_index("gx"), lax.axis_index("gy")
    y, z = lax.div(x, nz), lax.rem(x, nz)
    chip, core = lax.div(me, 2), lax.rem(me, 2)
    spot = chip * ny + y
    beside = around(n_gx, n_gy)
    merged = partners()
    mate = merged[1]
    rows_z = [(y * nz + lax.rem(z + k, nz), me) for k in range(1, nz)]
    rows_p, spots = [None], [None]
    for k in range(1, plane_size):
        other_c = lax.rem(chip + k // ny, nc)
        other_y = lax.rem(y + k % ny, ny)
        rows_p.append((other_y * nz + z, other_c * 2 + core))
        spots.append(other_c * ny + other_y)
    everyone = list(beside) + list(merged) + rows_z + rows_p[1:]
    rim = edges(n_gx, n_gy)
    low_half = lanes() < 64
    zero = jnp.zeros((64, 128), BF16)

    def send(source, target, sends, recvs, k, device):
        return pltpu.make_async_remote_copy(
            src_ref=source, dst_ref=target, send_sem=sends.at[k], recv_sem=recvs.at[k],
            device_id=device, device_id_type=MESH,
        )

    barrier = pltpu.get_barrier_semaphore()
    for device in everyone:
        pl.semaphore_signal(barrier, inc=1, device_id=device, device_id_type=MESH)

    def load(i):
        return pltpu.make_async_copy(
            features.at[pl.ds(2 * i, 2)], blocks.at[pl.ds(2 * i, 2)], load_s.at[i]
        )

    for i in range(4):
        load(i).start()
    grad_load = pltpu.make_async_copy(grad_in, grad_own, load_s.at[4])
    grad_load.start()
    weight_loads = [
        pltpu.make_async_copy(source, target, load_s.at[5 + k])
        for k, (source, target) in enumerate(((down_in, down), (conv_in, conv), (head_in, head)))
    ]
    for copy in weight_loads:
        copy.start()
    lane = lax.broadcasted_iota(jnp.int32, (8, 128), 1)
    values = jnp.full((8, 128), -1, jnp.int32)
    for k in range(8):
        values = jnp.where(lane == k, jnp.broadcast_to(maps[0, k], (8, 128)), values)
    table[...] = values
    for d in range(4):
        pool[d, 8] = zero
    for d in range(2):
        for j in range(4, 9):
            tall[d, j] = zero
    def pack(i, carry):
        load(i).wait()
        keep_a = flag(counts[0] - 2 * i) > 0
        keep_b = flag(counts[0] - 2 * i) > 1
        cols = [None] * 8
        for pq in range(4):
            a = jnp.where(keep_a, blocks[2 * i, :, pq * 128 : pq * 128 + 128], zero)
            b = jnp.where(keep_b, blocks[2 * i + 1, :, pq * 128 : pq * 128 + 128], zero)
            cols[2 * pq] = jnp.where(low_half, a, roll(b, 64))
            cols[2 * pq + 1] = jnp.where(low_half, roll(a, 64), b)
        for d in range(6):
            rows = pool.at[d, i] if d < 4 else tall.at[d - 4, i]
            rows[...] = pack_face(cols, d // 2, d % 2 == 0)
        for c in range(8):
            taps[i, 0:64, c * 128 : c * 128 + 128] = cols[c]
        return carry

    lax.fori_loop(0, 4, pack, 0, unroll=True)
    for copy in weight_loads:
        copy.wait()
    down_rows[...] = dot(selection(), down[...], 1, 1).astype(BF16)
    grad_load.wait()
    pl.semaphore_wait(barrier, len(everyone))
    face_copies = [
        send(pool.at[d, pl.ds(0, 4)], pool.at[d, pl.ds(4, 4)], face_s, face_r, d, beside[d]) for d in range(4)
    ] + [send(table, tables.at[m], face_s, face_r, 4 + m, merged[m]) for m in range(3)]
    for copy in face_copies:
        copy.start()

    def chunk(source, target, sends, recvs, i, leg):
        rows = (source if leg < 2 else target).at[pl.ds(2 * i, 2)]
        place = target.at[pl.ds(8 * leg + 2 * i, 2)]
        return send(rows, place, sends, recvs, 4 * leg + i, merged[0] if leg == 0 else mate)

    def grad_chunk(i, leg):
        return chunk(grad_own, grad_far, back_s, back_r, i, leg)

    def octant_chunk(i, leg):
        return chunk(octants, received, merge_s, merge_r, i, leg)

    for i in range(4):
        grad_chunk(i, 0).start()
        grad_chunk(i, 1).start()
    def tap(i, d):
        cols = [taps[i, 0:64, c * 128 : c * 128 + 128] for c in range(8)]
        e0 = link_of(links, 2 * i, d, rim)
        e1 = link_of(links, 2 * i + 1, d, rim)
        rows = pool.at[d] if d < 4 else tall.at[d - 4]
        face = jnp.where(
            low_half,
            pltpu.roll(rows[lax.div(e0, 2)], 64 * lax.rem(e0, 2), 1),
            pltpu.roll(rows[lax.div(e1, 2)], 64 - 64 * lax.rem(e1, 2), 1),
        )
        moved = (shift_minus if d % 2 == 0 else shift_plus)(cols, d // 2, face)
        for c in range(8):
            taps[i, 64 * (d + 1) : 64 * (d + 2), c * 128 : c * 128 + 128] = moved[c]

    def upright(i, carry):
        tap(i, 4)
        tap(i, 5)
        return carry

    lax.fori_loop(0, 4, upright, 0, unroll=True)
    for d in range(7):
        block = conv[:, d * 64 : d * 64 + 64].astype(F32)
        turned[:, d * 64 : d * 64 + 64] = block.T.astype(BF16)
    conv_acc[...] = jnp.zeros_like(conv_acc)
    down_acc[...] = jnp.zeros_like(down_acc)
    head_acc[...] = jnp.zeros_like(head_acc)
    for copy in face_copies:
        copy.wait()

    def level(i, carry):
        for d in range(4):
            tap(i, d)
        values = dot(conv[...], taps[i], 1, 0)
        hidden[i] = values
        active = (values * sigmoid(values)).astype(BF16)
        for c in range(8):
            act[i, c * 64 : c * 64 + 64, :] = active[:, c * 128 : c * 128 + 128]
        rows = dot(act[i], down_rows[...], 0, 0).astype(BF16)
        octants[2 * i] = rows[:64]
        octants[2 * i + 1] = rows[64:]
        octant_chunk(i, 0).start()
        octant_chunk(i, 1).start()
        grad_chunk(i, 0).wait_recv()
        grad_chunk(i, 2).start()
        return carry

    lax.fori_loop(0, 4, level, 0, unroll=True)
    for s in range(8):
        found = jnp.zeros((8, 128), jnp.int32)
        for m in range(4):
            entries = table[...] if m == 0 else tables[m - 1]
            found = jnp.where(entries == m * 8 + s, m * 8 + lane - 32, found)
        inverse[s] = jnp.clip(jnp.sum(found[0:1, :]) + 32, 0, 32)

    def settle(part):
        def rest(i, carry):
            part(i, 0).wait_send()
            part(i, 1).wait()
            part(i, 2).wait()
            return carry

        lax.fori_loop(0, 4, rest, 0)

    settle(grad_chunk)

    def merged_row(e, own, other):
        mine = own[jnp.clip(e, 0, 7)]
        theirs = other[jnp.clip(e - 8, 0, 23)]
        return jnp.where(flag(e) < 8, mine, jnp.where(flag(e) < 32, theirs, zero))

    def backward(i, carry):
        named = jnp.concatenate([
            merged_row(inverse[2 * i], grad_own, grad_far),
            merged_row(inverse[2 * i + 1], grad_own, grad_far),
        ], axis=0)
        values = jnp.concatenate([octants[2 * i], octants[2 * i + 1]], axis=0).astype(F32)
        s = sigmoid(values)
        active = (values * s).astype(BF16)
        head_acc[...] += dot(named, active, 0, 0)
        rows = dot(named, head[...], 1, 0) * (s * (1.0 + values * (1.0 - s)))
        rows = rows.astype(BF16)
        down_acc[...] += dot(act[i], rows, 1, 0)
        patch = dot(down_rows[...], rows, 1, 1)
        for c in range(8):
            slope = silu_grad(hidden[i, :, c * 128 : c * 128 + 128])
            value = (patch[c * 64 : c * 64 + 64] * slope).astype(BF16)
            hidden_grad[i, :, c * 128 : c * 128 + 128] = value
        conv_acc[...] += dot(hidden_grad[i], taps[i], 1, 1)
        return carry

    lax.fori_loop(0, 4, backward, 0, unroll=True)
    wide = conv_acc[...].astype(BF16)
    for j in range(3):
        grads[0, j * 64 : j * 64 + 64, :] = wide[:, j * 128 : j * 128 + 128]
    grads[0, 192:256, :] = jnp.concatenate([wide[:, 384:448], jnp.zeros((64, 64), BF16)], axis=1)
    ordered = dot(down_acc[...].astype(BF16), selection(), 0, 0).astype(BF16)
    for j in range(4):
        row = 256 + 128 * (j % 2) if j < 2 else 128 * (j % 2)
        grads[j // 2, row : row + 128, :] = ordered[:, j * 128 : j * 128 + 128]
    grads[1, 256:384, :] = head_acc[...].astype(BF16)
    grads[1, 384:512, :] = jnp.zeros((128, 128), BF16)
    copy_0 = send(grads.at[1 - core], part_0, send_0, recv_0, 0, mate)
    copy_0.start()

    def relay(i, carry):
        octant_chunk(i, 0).wait_recv()
        octant_chunk(i, 2).start()
        return carry

    lax.fori_loop(0, 4, relay, 0)

    def plane(i, carry):
        cols = [hidden_grad[i, :, c * 128 : c * 128 + 128] for c in range(8)]
        for d in range(6):
            face = pack_face(cols, d // 2, d % 2 == 1)
            planes[d, 0, i] = face.astype(F32)
            planes[d, 1, i] = roll(face, 64).astype(F32)
        return carry

    def gathered(d, j):
        out = jnp.zeros((64, 128), F32)
        for i in range(4):
            e0 = link_of(links, 2 * i, d, rim)
            e1 = link_of(links, 2 * i + 1, d, rim)
            straight = jnp.where(low_half, flag(e0), flag(e1 - 1))
            crossed = jnp.where(low_half, flag(e1), flag(e0 - 1))
            out = out + jnp.where(straight == 2 * j, planes[d, 0, i], 0.0)
            out = out + jnp.where(crossed == 2 * j, planes[d, 1, i], 0.0)
        return out

    def collect_far(j, carry):
        for d in range(4):
            far_out[d, j] = gathered(d, 4 + j).astype(BF16)
        return carry

    def collect_near(j, carry):
        for d in range(6):
            near[d, j] = gathered(d, j)
        return carry

    copy_0.wait()
    result = grads[core].astype(F32) + part_0[...].astype(F32)
    per = result.shape[0] // plane_size
    sum_0[...] = result.astype(BF16).reshape(plane_size, per, 128)
    copies_1 = [
        send(sum_0.at[spots[k]], part_1.at[k], send_1, recv_1, k, rows_p[k])
        for k in range(1, plane_size)
    ]
    for copy in copies_1:
        copy.start()
    lax.fori_loop(0, 4, plane, 0)
    lax.fori_loop(0, 4, collect_far, 0)
    target = (beside[1], beside[0], beside[3], beside[2])
    returns = [send(far_out.at[d], far_in.at[d], ret_s, ret_r, d, target[d]) for d in range(4)]
    for copy in returns:
        copy.start()
    for copy in copies_1:
        copy.wait()
    result = sum_0[spot].astype(F32)
    for k in range(1, plane_size):
        result = result + part_1[k].astype(F32)
    part_2[z] = result.astype(BF16)
    copies_2 = [
        send(part_2.at[z], part_2.at[z], send_2, recv_2, k, rows_z[k - 1]) for k in range(1, nz)
    ]
    for copy in copies_2:
        copy.start()
    settle(octant_chunk)
    for k in range(8):
        coarse[k * 64 : k * 64 + 64, :] = merged_row(maps[0, k], octants, received)
    values = coarse[...].astype(F32)
    active = (values * sigmoid(values)).astype(BF16)
    latent[...] = dot(active, head[...], 1, 1).astype(BF16)
    lax.fori_loop(0, 4, collect_near, 0)
    for copy in returns:
        copy.wait()

    def final(i, carry):
        cols = [hidden_grad[i, :, c * 128 : c * 128 + 128] for c in range(8)]
        for c in range(8):
            final_taps[0:64, c * 128 : c * 128 + 128] = cols[c]
        for d in range(6):
            face = near[d, i]
            if d < 4:
                face = face + far_in[d, i].astype(F32)
            moved = (shift_plus if d % 2 == 0 else shift_minus)(cols, d // 2, face.astype(BF16))
            for c in range(8):
                final_taps[64 * (d + 1) : 64 * (d + 2), c * 128 : c * 128 + 128] = moved[c]
        values = dot(turned[...], final_taps[...], 1, 0)
        keep_a = flag(counts[0] - 2 * i) > 0
        keep_b = flag(counts[0] - 2 * i) > 1
        for pq in range(4):
            even = values[:, pq * 256 : pq * 256 + 128]
            odd = values[:, pq * 256 + 128 : pq * 256 + 256]
            a = jnp.where(low_half, even, roll(odd, 64))
            b = jnp.where(low_half, roll(even, 64), odd)
            spread = slice(pq * 128, pq * 128 + 128)
            out[2 * i, :, spread] = jnp.where(keep_a, a, 0.0).astype(BF16)
            out[2 * i + 1, :, spread] = jnp.where(keep_b, b, 0.0).astype(BF16)
        return carry

    for copy in copies_2:
        copy.wait()
    result = part_2[0].astype(F32)
    for k in range(1, nz):
        result = result + part_2[k].astype(F32)
    part_3[spot] = result.astype(BF16)
    copies_3 = [
        send(part_3.at[spot], part_3.at[spot], send_3, recv_3, k, rows_p[k])
        for k in range(1, plane_size)
    ]
    for copy in copies_3:
        copy.start()
    lax.fori_loop(0, 4, final, 0, unroll=True)
    for copy in copies_3:
        copy.wait()
    copy_4 = send(part_3, total.at[core], send_4, recv_4, 0, mate)
    copy_4.start()
    total[core] = part_3[...]
    copy_4.wait()


def unpack_kernel(
    latent, features, total, latent_out, features_out, conv_out, down_out, head_out,
    conv_hold, down_hold, head_hold, store_s,
):
    scale = float(2048) ** -0.5
    moves = [(features, features_out), (latent, latent_out.at[0])]
    moves += [(conv_hold, conv_out), (down_hold, down_out), (head_hold, head_out)]
    stores = [
        pltpu.make_async_copy(source, target, store_s.at[k])
        for k, (source, target) in enumerate(moves)
    ]
    stores[0].start()
    stores[1].start()
    rows = total[...].reshape(GRAD_ROWS, 128)

    def scaled(first, last):
        return rows[first:last].astype(F32) * scale

    for j in range(4):
        down_hold[:, j * 128 : j * 128 + 128] = scaled(256 + j * 128, 384 + j * 128)
    stores[3].start()
    for j in range(3):
        conv_hold[:, j * 128 : j * 128 + 128] = scaled(j * 64, j * 64 + 64)
    conv_hold[:, 384:448] = scaled(192, 256)[:, :64]
    stores[2].start()
    head_hold[...] = scaled(768, 896)
    stores[4].start()
    for store in stores:
        store.wait()


VM = pl.BlockSpec(memory_space=pltpu.VMEM)
SM = pl.BlockSpec(memory_space=pltpu.SMEM)
ANY = pl.BlockSpec(memory_space=pl.ANY)
HBM = pl.BlockSpec(memory_space=pltpu.HBM)
DMA = pltpu.SemaphoreType.DMA
VMEM = pltpu.VMEM


def shape(*dims, dtype=BF16):
    return jax.ShapeDtypeStruct(dims, dtype)


def bind(kernel, *fixed):
    def run(*refs):
        kernel(*fixed, *refs)

    return run


def body(
    features, neighbours, counts, conv_weight, down_weight, head_weight, coarse_map, latent_grad
):
    n_gx, n_gy = lax.axis_size("gx"), lax.axis_size("gy")
    nz = ring_z(n_gx)
    spots = (n_gx // nz) * (n_gy // 2)
    per = GRAD_ROWS // 2 // spots
    pairs = [DMA((1,)), DMA((spots,)), DMA((nz,)), DMA((spots,)), DMA((1,))]
    latent, grad, total = pl.pallas_call(
        bind(step_kernel, n_gx, n_gy), name="step", in_specs=[SM] * 3 + [HBM] * 5,
        out_specs=[VM] * 3,
        out_shape=[shape(512, 128), shape(8, 64, 512), shape(2, spots, per, 128)],
        scratch_shapes=[
            VMEM((64, 448), BF16), VMEM((128, 512), BF16), VMEM((128, 128), BF16),
            VMEM((8, 64, 512), BF16), VMEM((8, 64, 128), BF16), VMEM((24, 64, 128), BF16),
            VMEM((8, 128), jnp.int32), VMEM((3, 8, 128), jnp.int32),
            VMEM((512, 128), BF16), VMEM((64, 448), BF16), VMEM((4, 9, 64, 128), BF16), VMEM((2, 9, 64, 128), BF16),
            VMEM((4, 448, 1024), BF16), VMEM((4, 64, 1024), F32), VMEM((4, 512, 128), BF16),
            VMEM((8, 64, 128), BF16), VMEM((24, 64, 128), BF16),
            pltpu.SMEM((8,), jnp.int32), VMEM((4, 64, 1024), BF16), VMEM((6, 2, 4, 64, 128), F32),
            VMEM((6, 4, 64, 128), F32), VMEM((4, 4, 64, 128), BF16), VMEM((4, 4, 64, 128), BF16),
            VMEM((64, 448), F32), VMEM((512, 128), F32), VMEM((128, 128), F32),
            VMEM((448, 1024), BF16), VMEM((512, 128), BF16),
            VMEM((2, 512, 128), BF16), VMEM((512, 128), BF16), VMEM((spots, per, 128), BF16),
            VMEM((spots, per, 128), BF16), VMEM((nz, per, 128), BF16), VMEM((spots, per, 128), BF16),
            DMA((8,)),
            DMA((7,)), DMA((7,)), DMA((12,)), DMA((12,)), DMA((12,)), DMA((12,)),
            DMA((4,)), DMA((4,)),
        ] + [pair for pair in pairs for _ in range(2)],
        compiler_params=pltpu.CompilerParams(
            collective_id=0, has_side_effects=True, vmem_limit_bytes=20 * 2**20
        ),
    )(
        counts, *[
            pltpu.with_memory_space_constraint(value, pltpu.HBM)
            for value in (
                neighbours, coarse_map, conv_weight, down_weight, head_weight, features,
                latent_grad.reshape(8, 64, 128),
            )
        ],
    )
    return pl.pallas_call(
        unpack_kernel, name="unpack", in_specs=[VM] * 3, out_specs=[ANY] * 5,
        out_shape=[
            shape(1, 512, 128), shape(8, 64, 512), shape(64, 448, dtype=F32),
            shape(128, 512, dtype=F32), shape(128, 128, dtype=F32),
        ],
        scratch_shapes=[
            VMEM((64, 448), F32), VMEM((128, 512), F32), VMEM((128, 128), F32), DMA((5,)),
        ],
        compiler_params=pltpu.CompilerParams(vmem_limit_bytes=8 * 2**20),
    )(latent, grad, total)


def solution(mesh):
    placed = (
        P(("gx", "gy"), None, None),
        P(("gx", "gy"), None),
        P(("gx", "gy")),
        P(),
        P(),
        P(),
        P(("gx", "gy"), None),
        P(("gx", "gy"), None, None),
    )
    return jax.shard_map(
        body,
        mesh=mesh,
        in_specs=placed,
        out_specs=(P(("gx", "gy"), None, None), P(("gx", "gy"), None, None), P(), P(), P()),
        check_vma=False,
    )
```

```python
import jax
import jax.numpy as jnp
from jax import lax
from jax.experimental import pallas as pl
from jax.experimental.pallas import tpu as pltpu
from jax.sharding import PartitionSpec as P

MESH = pl.DeviceIdType.MESH
F32 = jnp.float32
BF16 = jnp.bfloat16
STRIDE = (16, 4, 1)
GRAD_ROWS = 1024


def ring_z(n_gx):
    return 8 if n_gx % 8 == 0 else n_gx // 2


def dot(a, b, ca, cb):
    return lax.dot_general(a, b, (((ca,), (cb,)), ((), ())), preferred_element_type=F32)


def lanes():
    return lax.broadcasted_iota(jnp.int32, (64, 128), 1)


def flag(value):
    return jnp.broadcast_to(value, (64, 128))


def roll(values, amount):
    amount = amount % 128
    return values if amount == 0 else pltpu.roll(values, amount, 1)


def column(axis, bit, s):
    high, low = s // 2, s % 2
    bits = [high, low]
    bits.insert(axis, bit)
    return bits[0] * 4 + bits[1] * 2 + bits[2]


def field(axis):
    return lax.rem(lax.div(lanes(), STRIDE[axis]), 4)


def pack_face(cols, axis, upper):
    step = STRIDE[axis]
    place = field(axis)
    out = None
    for s in range(4):
        shift = step * (s - 3) if upper else step * s
        moved = roll(cols[column(axis, int(upper), s)], shift)
        out = moved if out is None else jnp.where(place == s, moved, out)
    return out


def shift_minus(cols, axis, face):
    step = STRIDE[axis]
    edge = field(axis) == 0
    out = [None] * 8
    for s in range(4):
        low, high = column(axis, 0, s), column(axis, 1, s)
        out[high] = cols[low]
        out[low] = jnp.where(edge, roll(face, -step * s), roll(cols[high], step))
    return out


def shift_plus(cols, axis, face):
    step = STRIDE[axis]
    edge = field(axis) == 3
    out = [None] * 8
    for s in range(4):
        low, high = column(axis, 0, s), column(axis, 1, s)
        out[low] = cols[high]
        out[high] = jnp.where(edge, roll(face, step * (3 - s)), roll(cols[low], -step))
    return out


def sigmoid(values):
    return 1.0 / (1.0 + jnp.exp(-values))


def edges(n_gx, n_gy):
    x, y = lax.axis_index("gx"), lax.axis_index("gy")
    return (x == 0, x == n_gx - 1, y == 0, y == n_gy - 1)


def link_of(links, slot, direction, rim):
    value = links[slot, direction]
    if direction < 4:
        return jnp.where(jnp.logical_and(rim[direction], value >= 8), 16, value)
    return value


def selection():
    row = lax.broadcasted_iota(jnp.int32, (512, 512), 0)
    col = lax.broadcasted_iota(jnp.int32, (512, 512), 1)
    return jnp.where(col == lax.rem(row, 64) * 8 + lax.div(row, 64), 1.0, 0.0).astype(BF16)


def around(n_gx, n_gy):
    x, y = lax.axis_index("gx"), lax.axis_index("gy")
    return (
        (lax.rem(x + 1, n_gx), y),
        (lax.rem(x + n_gx - 1, n_gx), y),
        (x, lax.rem(y + 1, n_gy)),
        (x, lax.rem(y + n_gy - 1, n_gy)),
    )


def partners():
    x, y = lax.axis_index("gx"), lax.axis_index("gy")
    x1 = x + 1 - 2 * lax.rem(x, 2)
    y1 = y + 1 - 2 * lax.rem(y, 2)
    return ((x1, y), (x, y1), (x1, y1))


def step_kernel(
    n_gx, n_gy, counts, links, maps, conv_in, down_in, head_in, features, grad_in,
    latent, out, total,
    conv, down, head, blocks, grad_own, grad_far, table, tables, down_rows, turned, pool, tall, taps, slope,
    act, octants, received, inverse, hidden_grad, planes, near, far_out, far_in, conv_acc, down_acc,
    head_acc, final_taps, coarse,
    grads, part_0, sum_0, part_1, part_2, part_3,
    known, load_s, face_s, face_r, merge_s, merge_r, back_s, back_r, ret_s, ret_r,
    send_0, recv_0, send_1, recv_1, send_2, recv_2, send_3, recv_3, send_4, recv_4,
):
    nz = ring_z(n_gx)
    ny, nc = n_gx // nz, n_gy // 2
    plane_size = nc * ny
    x, me = lax.axis_index("gx"), lax.axis_index("gy")
    y, z = lax.div(x, nz), lax.rem(x, nz)
    chip, core = lax.div(me, 2), lax.rem(me, 2)
    spot = chip * ny + y
    beside = around(n_gx, n_gy)
    merged = partners()
    mate = merged[1]
    rows_z = [(y * nz + lax.rem(z + k, nz), me) for k in range(1, nz)]
    rows_p, spots = [None], [None]
    for k in range(1, plane_size):
        other_c = lax.rem(chip + k // ny, nc)
        other_y = lax.rem(y + k % ny, ny)
        rows_p.append((other_y * nz + z, other_c * 2 + core))
        spots.append(other_c * ny + other_y)
    ring = [
        (y * nz + lax.rem(z + 1, nz), me), (y * nz + lax.rem(z + nz - 1, nz), me),
        (lax.rem(y + 1, ny) * nz + z, me), (lax.rem(y + ny - 1, ny) * nz + z, me),
        (x, lax.rem(chip + 1, nc) * 2 + core), (x, lax.rem(chip + nc - 1, nc) * 2 + core),
    ]
    everyone = list(beside) + list(merged) + ring

    def tell(number):
        for device in ring:
            pl.semaphore_signal(known.at[number], inc=1, device_id=device, device_id_type=MESH)

    def hear(number):
        pl.semaphore_wait(known.at[number], len(ring))

    rim = edges(n_gx, n_gy)
    low_half = lanes() < 64
    zero = jnp.zeros((64, 128), BF16)

    def send(source, target, sends, recvs, k, device):
        return pltpu.make_async_remote_copy(
            src_ref=source, dst_ref=target, send_sem=sends.at[k], recv_sem=recvs.at[k],
            device_id=device, device_id_type=MESH,
        )

    barrier = pltpu.get_barrier_semaphore()
    for device in everyone:
        pl.semaphore_signal(barrier, inc=1, device_id=device, device_id_type=MESH)

    def load(i):
        return pltpu.make_async_copy(
            features.at[pl.ds(2 * i, 2)], blocks.at[pl.ds(2 * i, 2)], load_s.at[i]
        )

    for i in range(4):
        load(i).start()
    grad_load = pltpu.make_async_copy(grad_in, grad_own, load_s.at[4])
    grad_load.start()
    weight_loads = [
        pltpu.make_async_copy(source, target, load_s.at[5 + k])
        for k, (source, target) in enumerate(((down_in, down), (conv_in, conv), (head_in, head)))
    ]
    for copy in weight_loads:
        copy.start()
    lane = lax.broadcasted_iota(jnp.int32, (8, 128), 1)
    values = jnp.full((8, 128), -1, jnp.int32)
    for k in range(8):
        values = jnp.where(lane == k, jnp.broadcast_to(maps[0, k], (8, 128)), values)
    table[...] = values
    for d in range(4):
        pool[d, 8] = zero
    for d in range(2):
        for j in range(4, 9):
            tall[d, j] = zero
    def pack(i, carry):
        load(i).wait()
        keep_a = flag(counts[0] - 2 * i) > 0
        keep_b = flag(counts[0] - 2 * i) > 1
        cols = [None] * 8
        for pq in range(4):
            a = jnp.where(keep_a, blocks[2 * i, :, pq * 128 : pq * 128 + 128], zero)
            b = jnp.where(keep_b, blocks[2 * i + 1, :, pq * 128 : pq * 128 + 128], zero)
            cols[2 * pq] = jnp.where(low_half, a, roll(b, 64))
            cols[2 * pq + 1] = jnp.where(low_half, roll(a, 64), b)
        for d in range(6):
            rows = pool.at[d, i] if d < 4 else tall.at[d - 4, i]
            rows[...] = pack_face(cols, d // 2, d % 2 == 0)
        for c in range(8):
            taps[i, 0:64, c * 128 : c * 128 + 128] = cols[c]
        return carry

    lax.fori_loop(0, 4, pack, 0, unroll=True)
    for copy in weight_loads:
        copy.wait()
    down_rows[...] = dot(selection(), down[...], 1, 1).astype(BF16)
    grad_load.wait()
    pl.semaphore_wait(barrier, len(everyone))
    tell(0)
    face_copies = [
        send(pool.at[d, pl.ds(0, 4)], pool.at[d, pl.ds(4, 4)], face_s, face_r, d, beside[d]) for d in range(4)
    ] + [send(table, tables.at[m], face_s, face_r, 4 + m, merged[m]) for m in range(3)]
    for copy in face_copies:
        copy.start()

    def chunk(source, target, sends, recvs, i, leg):
        rows = (source if leg < 2 else target).at[pl.ds(2 * i, 2)]
        place = target.at[pl.ds(8 * leg + 2 * i, 2)]
        return send(rows, place, sends, recvs, 4 * leg + i, merged[0] if leg == 0 else mate)

    def grad_chunk(i, leg):
        return chunk(grad_own, grad_far, back_s, back_r, i, leg)

    def octant_chunk(i, leg):
        return chunk(octants, received, merge_s, merge_r, i, leg)

    for i in range(4):
        grad_chunk(i, 0).start()
        grad_chunk(i, 1).start()
    def tap(i, d):
        cols = [taps[i, 0:64, c * 128 : c * 128 + 128] for c in range(8)]
        e0 = link_of(links, 2 * i, d, rim)
        e1 = link_of(links, 2 * i + 1, d, rim)
        rows = pool.at[d] if d < 4 else tall.at[d - 4]
        face = jnp.where(
            low_half,
            pltpu.roll(rows[lax.div(e0, 2)], 64 * lax.rem(e0, 2), 1),
            pltpu.roll(rows[lax.div(e1, 2)], 64 - 64 * lax.rem(e1, 2), 1),
        )
        moved = (shift_minus if d % 2 == 0 else shift_plus)(cols, d // 2, face)
        for c in range(8):
            taps[i, 64 * (d + 1) : 64 * (d + 2), c * 128 : c * 128 + 128] = moved[c]

    def upright(i, carry):
        tap(i, 4)
        tap(i, 5)
        return carry

    lax.fori_loop(0, 4, upright, 0, unroll=True)
    for d in range(7):
        block = conv[:, d * 64 : d * 64 + 64].astype(F32)
        turned[:, d * 64 : d * 64 + 64] = block.T.astype(BF16)
    conv_acc[...] = jnp.zeros_like(conv_acc)
    down_acc[...] = jnp.zeros_like(down_acc)
    head_acc[...] = jnp.zeros_like(head_acc)
    for copy in face_copies:
        copy.wait()
    hear(0)
    tell(1)

    def level(i, carry):
        for d in range(4):
            tap(i, d)
        values = dot(conv[...], taps[i], 1, 0)
        s = sigmoid(values)
        slope[i] = s * (1.0 + values * (1.0 - s))
        active = (values * s).astype(BF16)
        for c in range(8):
            act[i, c * 64 : c * 64 + 64, :] = active[:, c * 128 : c * 128 + 128]
        rows = dot(act[i], down_rows[...], 0, 0).astype(BF16)
        octants[2 * i] = rows[:64]
        octants[2 * i + 1] = rows[64:]
        grad_chunk(i, 0).wait_recv()
        grad_chunk(i, 2).start()
        return carry

    lax.fori_loop(0, 4, level, 0, unroll=True)
    for s in range(8):
        found = jnp.zeros((8, 128), jnp.int32)
        for m in range(4):
            entries = table[...] if m == 0 else tables[m - 1]
            found = jnp.where(entries == m * 8 + s, m * 8 + lane - 32, found)
        inverse[s] = jnp.clip(jnp.sum(found[0:1, :]) + 32, 0, 32)

    def settle(part):
        def rest(i, carry):
            part(i, 0).wait_send()
            part(i, 1).wait()
            part(i, 2).wait()
            return carry

        lax.fori_loop(0, 4, rest, 0)

    hear(1)
    tell(2)
    settle(grad_chunk)

    def merged_row(e, own, other):
        mine = own[jnp.clip(e, 0, 7)]
        theirs = other[jnp.clip(e - 8, 0, 23)]
        return jnp.where(flag(e) < 8, mine, jnp.where(flag(e) < 32, theirs, zero))

    def backward(i, carry):
        named = jnp.concatenate([
            merged_row(inverse[2 * i], grad_own, grad_far),
            merged_row(inverse[2 * i + 1], grad_own, grad_far),
        ], axis=0)
        values = jnp.concatenate([octants[2 * i], octants[2 * i + 1]], axis=0).astype(F32)
        s = sigmoid(values)
        active = (values * s).astype(BF16)
        head_acc[...] += dot(named, active, 0, 0)
        rows = dot(named, head[...], 1, 0) * (s * (1.0 + values * (1.0 - s)))
        rows = rows.astype(BF16)
        down_acc[...] += dot(act[i], rows, 1, 0)
        patch = dot(down_rows[...], rows, 1, 1)
        for c in range(8):
            factor = slope[i, :, c * 128 : c * 128 + 128]
            value = (patch[c * 64 : c * 64 + 64] * factor).astype(BF16)
            hidden_grad[i, :, c * 128 : c * 128 + 128] = value
        conv_acc[...] += dot(hidden_grad[i], taps[i], 1, 1)
        return carry

    lax.fori_loop(0, 4, backward, 0, unroll=True)
    wide = conv_acc[...].astype(BF16)
    for j in range(3):
        grads[0, j * 64 : j * 64 + 64, :] = wide[:, j * 128 : j * 128 + 128]
    grads[0, 192:256, :] = jnp.concatenate([wide[:, 384:448], jnp.zeros((64, 64), BF16)], axis=1)
    ordered = dot(down_acc[...].astype(BF16), selection(), 0, 0).astype(BF16)
    for j in range(4):
        row = 256 + 128 * (j % 2) if j < 2 else 128 * (j % 2)
        grads[j // 2, row : row + 128, :] = ordered[:, j * 128 : j * 128 + 128]
    grads[1, 256:384, :] = head_acc[...].astype(BF16)
    grads[1, 384:512, :] = jnp.zeros((128, 128), BF16)
    copy_0 = send(grads.at[1 - core], part_0, send_0, recv_0, 0, mate)
    copy_0.start()

    for i in range(4):
        octant_chunk(i, 0).start()
        octant_chunk(i, 1).start()

    def plane(i, carry):
        cols = [hidden_grad[i, :, c * 128 : c * 128 + 128] for c in range(8)]
        for d in range(6):
            face = pack_face(cols, d // 2, d % 2 == 1)
            planes[d, 0, i] = face.astype(F32)
            planes[d, 1, i] = roll(face, 64).astype(F32)
        return carry

    def gathered(d, j):
        out = jnp.zeros((64, 128), F32)
        for i in range(4):
            e0 = link_of(links, 2 * i, d, rim)
            e1 = link_of(links, 2 * i + 1, d, rim)
            straight = jnp.where(low_half, flag(e0), flag(e1 - 1))
            crossed = jnp.where(low_half, flag(e1), flag(e0 - 1))
            out = out + jnp.where(straight == 2 * j, planes[d, 0, i], 0.0)
            out = out + jnp.where(crossed == 2 * j, planes[d, 1, i], 0.0)
        return out

    def collect_far(j, carry):
        for d in range(4):
            far_out[d, j] = gathered(d, 4 + j).astype(BF16)
        return carry

    def collect_near(j, carry):
        for d in range(6):
            near[d, j] = gathered(d, j)
        return carry

    copy_0.wait()
    result = grads[core].astype(F32) + part_0[...].astype(F32)
    per = result.shape[0] // plane_size
    sum_0[...] = result.astype(BF16).reshape(plane_size, per, 128)
    hear(2)
    copies_1 = [
        send(sum_0.at[spots[k]], part_1.at[k], send_1, recv_1, k, rows_p[k])
        for k in range(1, plane_size)
    ]
    for copy in copies_1:
        copy.start()
    lax.fori_loop(0, 4, plane, 0)
    lax.fori_loop(0, 4, collect_far, 0)
    target = (beside[1], beside[0], beside[3], beside[2])
    returns = [send(far_out.at[d], far_in.at[d], ret_s, ret_r, d, target[d]) for d in range(4)]
    for copy in returns:
        copy.start()
    for copy in copies_1:
        copy.wait()
    result = sum_0[spot].astype(F32)
    for k in range(1, plane_size):
        result = result + part_1[k].astype(F32)
    part_2[z] = result.astype(BF16)
    copies_2 = [
        send(part_2.at[z], part_2.at[z], send_2, recv_2, k, rows_z[k - 1]) for k in range(1, nz)
    ]
    for copy in copies_2:
        copy.start()
    def relay(i, carry):
        octant_chunk(i, 0).wait_recv()
        octant_chunk(i, 2).start()
        return carry

    lax.fori_loop(0, 4, relay, 0)

    lax.fori_loop(0, 4, collect_near, 0)
    for copy in returns:
        copy.wait()

    def final(i, carry):
        cols = [hidden_grad[i, :, c * 128 : c * 128 + 128] for c in range(8)]
        for c in range(8):
            final_taps[0:64, c * 128 : c * 128 + 128] = cols[c]
        for d in range(6):
            face = near[d, i]
            if d < 4:
                face = face + far_in[d, i].astype(F32)
            moved = (shift_plus if d % 2 == 0 else shift_minus)(cols, d // 2, face.astype(BF16))
            for c in range(8):
                final_taps[64 * (d + 1) : 64 * (d + 2), c * 128 : c * 128 + 128] = moved[c]
        values = dot(turned[...], final_taps[...], 1, 0)
        keep_a = flag(counts[0] - 2 * i) > 0
        keep_b = flag(counts[0] - 2 * i) > 1
        for pq in range(4):
            even = values[:, pq * 256 : pq * 256 + 128]
            odd = values[:, pq * 256 + 128 : pq * 256 + 256]
            a = jnp.where(low_half, even, roll(odd, 64))
            b = jnp.where(low_half, roll(even, 64), odd)
            spread = slice(pq * 128, pq * 128 + 128)
            out[2 * i, :, spread] = jnp.where(keep_a, a, 0.0).astype(BF16)
            out[2 * i + 1, :, spread] = jnp.where(keep_b, b, 0.0).astype(BF16)
        return carry

    lax.fori_loop(0, 4, final, 0, unroll=True)
    for copy in copies_2:
        copy.wait()
    result = part_2[0].astype(F32)
    for k in range(1, nz):
        result = result + part_2[k].astype(F32)
    part_3[spot] = result.astype(BF16)
    copies_3 = [
        send(part_3.at[spot], part_3.at[spot], send_3, recv_3, k, rows_p[k])
        for k in range(1, plane_size)
    ]
    for copy in copies_3:
        copy.start()

    def across(k):
        origin = lax.rem(chip + nc - k // ny, nc) * ny + lax.rem(y + ny - k % ny, ny)
        return send(part_3.at[origin], total.at[core, origin], send_4, recv_4, k, mate)

    def hops(k):
        return min(k // ny, nc - k // ny) + min(k % ny, ny - k % ny)

    nearest = sorted(range(plane_size), key=hops)
    copies_4 = [across(0)]
    copies_4[0].start()
    settle(octant_chunk)
    for k in range(8):
        coarse[k * 64 : k * 64 + 64, :] = merged_row(maps[0, k], octants, received)
    values = coarse[...].astype(F32)
    active = (values * sigmoid(values)).astype(BF16)
    latent[...] = dot(active, head[...], 1, 1).astype(BF16)
    for k in nearest[1:]:
        copies_3[k - 1].wait_recv()
        copies_4.append(across(k))
        copies_4[-1].start()
    for copy in copies_3:
        copy.wait_send()
    total[core] = part_3[...]
    for copy in copies_4:
        copy.wait()


def unpack_kernel(
    latent, features, total, latent_out, features_out, conv_out, down_out, head_out,
    conv_hold, down_hold, head_hold, store_s,
):
    scale = float(2048) ** -0.5
    moves = [(features, features_out), (latent, latent_out.at[0])]
    moves += [(conv_hold, conv_out), (down_hold, down_out), (head_hold, head_out)]
    stores = [
        pltpu.make_async_copy(source, target, store_s.at[k])
        for k, (source, target) in enumerate(moves)
    ]
    stores[0].start()
    stores[1].start()
    rows = total[...].reshape(GRAD_ROWS, 128)

    def scaled(first, last):
        return rows[first:last].astype(F32) * scale

    for j in range(4):
        down_hold[:, j * 128 : j * 128 + 128] = scaled(256 + j * 128, 384 + j * 128)
    stores[3].start()
    for j in range(3):
        conv_hold[:, j * 128 : j * 128 + 128] = scaled(j * 64, j * 64 + 64)
    conv_hold[:, 384:448] = scaled(192, 256)[:, :64]
    stores[2].start()
    head_hold[...] = scaled(768, 896)
    stores[4].start()
    for store in stores:
        store.wait()


VM = pl.BlockSpec(memory_space=pltpu.VMEM)
SM = pl.BlockSpec(memory_space=pltpu.SMEM)
ANY = pl.BlockSpec(memory_space=pl.ANY)
HBM = pl.BlockSpec(memory_space=pltpu.HBM)
DMA = pltpu.SemaphoreType.DMA
VMEM = pltpu.VMEM


def shape(*dims, dtype=BF16):
    return jax.ShapeDtypeStruct(dims, dtype)


def bind(kernel, *fixed):
    def run(*refs):
        kernel(*fixed, *refs)

    return run


def body(
    features, neighbours, counts, conv_weight, down_weight, head_weight, coarse_map, latent_grad
):
    n_gx, n_gy = lax.axis_size("gx"), lax.axis_size("gy")
    nz = ring_z(n_gx)
    spots = (n_gx // nz) * (n_gy // 2)
    per = GRAD_ROWS // 2 // spots
    pairs = [DMA((1,)), DMA((spots,)), DMA((nz,)), DMA((spots,)), DMA((spots,))]
    latent, grad, total = pl.pallas_call(
        bind(step_kernel, n_gx, n_gy), name="step", in_specs=[SM] * 3 + [HBM] * 5,
        out_specs=[VM] * 3,
        out_shape=[shape(512, 128), shape(8, 64, 512), shape(2, spots, per, 128)],
        scratch_shapes=[
            VMEM((64, 448), BF16), VMEM((128, 512), BF16), VMEM((128, 128), BF16),
            VMEM((8, 64, 512), BF16), VMEM((8, 64, 128), BF16), VMEM((24, 64, 128), BF16),
            VMEM((8, 128), jnp.int32), VMEM((3, 8, 128), jnp.int32),
            VMEM((512, 128), BF16), VMEM((64, 448), BF16), VMEM((4, 9, 64, 128), BF16), VMEM((2, 9, 64, 128), BF16),
            VMEM((4, 448, 1024), BF16), VMEM((4, 64, 1024), F32), VMEM((4, 512, 128), BF16),
            VMEM((8, 64, 128), BF16), VMEM((24, 64, 128), BF16),
            pltpu.SMEM((8,), jnp.int32), VMEM((4, 64, 1024), BF16), VMEM((6, 2, 4, 64, 128), F32),
            VMEM((6, 4, 64, 128), F32), VMEM((4, 4, 64, 128), BF16), VMEM((4, 4, 64, 128), BF16),
            VMEM((64, 448), F32), VMEM((512, 128), F32), VMEM((128, 128), F32),
            VMEM((448, 1024), BF16), VMEM((512, 128), BF16),
            VMEM((2, 512, 128), BF16), VMEM((512, 128), BF16), VMEM((spots, per, 128), BF16),
            VMEM((spots, per, 128), BF16), VMEM((nz, per, 128), BF16), VMEM((spots, per, 128), BF16),
            pltpu.SemaphoreType.REGULAR((3,)), DMA((8,)),
            DMA((7,)), DMA((7,)), DMA((12,)), DMA((12,)), DMA((12,)), DMA((12,)),
            DMA((4,)), DMA((4,)),
        ] + [pair for pair in pairs for _ in range(2)],
        compiler_params=pltpu.CompilerParams(
            collective_id=0, has_side_effects=True, vmem_limit_bytes=20 * 2**20
        ),
    )(
        counts, *[
            pltpu.with_memory_space_constraint(value, pltpu.HBM)
            for value in (
                neighbours, coarse_map, conv_weight, down_weight, head_weight, features,
                latent_grad.reshape(8, 64, 128),
            )
        ],
    )
    return pl.pallas_call(
        unpack_kernel, name="unpack", in_specs=[VM] * 3, out_specs=[ANY] * 5,
        out_shape=[
            shape(1, 512, 128), shape(8, 64, 512), shape(64, 448, dtype=F32),
            shape(128, 512, dtype=F32), shape(128, 128, dtype=F32),
        ],
        scratch_shapes=[
            VMEM((64, 448), F32), VMEM((128, 512), F32), VMEM((128, 128), F32), DMA((5,)),
        ],
        compiler_params=pltpu.CompilerParams(vmem_limit_bytes=8 * 2**20),
    )(latent, grad, total)


def solution(mesh):
    placed = (
        P(("gx", "gy"), None, None),
        P(("gx", "gy"), None),
        P(("gx", "gy")),
        P(),
        P(),
        P(),
        P(("gx", "gy"), None),
        P(("gx", "gy"), None, None),
    )
    return jax.shard_map(
        body,
        mesh=mesh,
        in_specs=placed,
        out_specs=(P(("gx", "gy"), None, None), P(("gx", "gy"), None, None), P(), P(), P()),
        check_vma=False,
    )
```

```python
import jax
import jax.numpy as jnp
from jax import lax
from jax.experimental import pallas as pl
from jax.experimental.pallas import tpu as pltpu
from jax.sharding import PartitionSpec as P

MESH = pl.DeviceIdType.MESH
F32 = jnp.float32
BF16 = jnp.bfloat16
STRIDE = (16, 4, 1)
GRAD_ROWS = 1024


def ring_z(n_gx):
    return 8 if n_gx % 8 == 0 else n_gx // 2


def dot(a, b, ca, cb):
    return lax.dot_general(a, b, (((ca,), (cb,)), ((), ())), preferred_element_type=F32)


def lanes():
    return lax.broadcasted_iota(jnp.int32, (64, 128), 1)


def flag(value):
    return jnp.broadcast_to(value, (64, 128))


def roll(values, amount):
    amount = amount % 128
    return values if amount == 0 else pltpu.roll(values, amount, 1)


def column(axis, bit, s):
    high, low = s // 2, s % 2
    bits = [high, low]
    bits.insert(axis, bit)
    return bits[0] * 4 + bits[1] * 2 + bits[2]


def field(axis):
    return lax.rem(lax.div(lanes(), STRIDE[axis]), 4)


def pack_face(cols, axis, upper):
    step = STRIDE[axis]
    place = field(axis)
    out = None
    for s in range(4):
        shift = step * (s - 3) if upper else step * s
        moved = roll(cols[column(axis, int(upper), s)], shift)
        out = moved if out is None else jnp.where(place == s, moved, out)
    return out


def shift_minus(cols, axis, face):
    step = STRIDE[axis]
    edge = field(axis) == 0
    out = [None] * 8
    for s in range(4):
        low, high = column(axis, 0, s), column(axis, 1, s)
        out[high] = cols[low]
        out[low] = jnp.where(edge, roll(face, -step * s), roll(cols[high], step))
    return out


def shift_plus(cols, axis, face):
    step = STRIDE[axis]
    edge = field(axis) == 3
    out = [None] * 8
    for s in range(4):
        low, high = column(axis, 0, s), column(axis, 1, s)
        out[low] = cols[high]
        out[high] = jnp.where(edge, roll(face, step * (3 - s)), roll(cols[low], -step))
    return out


def sigmoid(values):
    return 1.0 / (1.0 + jnp.exp(-values))


def edges(n_gx, n_gy):
    x, y = lax.axis_index("gx"), lax.axis_index("gy")
    return (x == 0, x == n_gx - 1, y == 0, y == n_gy - 1)


def link_of(links, slot, direction, rim):
    value = links[slot, direction]
    if direction < 4:
        return jnp.where(jnp.logical_and(rim[direction], value >= 8), 16, value)
    return value


def selection():
    row = lax.broadcasted_iota(jnp.int32, (512, 512), 0)
    col = lax.broadcasted_iota(jnp.int32, (512, 512), 1)
    return jnp.where(col == lax.rem(row, 64) * 8 + lax.div(row, 64), 1.0, 0.0).astype(BF16)


def around(n_gx, n_gy):
    x, y = lax.axis_index("gx"), lax.axis_index("gy")
    return (
        (lax.rem(x + 1, n_gx), y),
        (lax.rem(x + n_gx - 1, n_gx), y),
        (x, lax.rem(y + 1, n_gy)),
        (x, lax.rem(y + n_gy - 1, n_gy)),
    )


def partners():
    x, y = lax.axis_index("gx"), lax.axis_index("gy")
    x1 = x + 1 - 2 * lax.rem(x, 2)
    y1 = y + 1 - 2 * lax.rem(y, 2)
    return ((x1, y), (x, y1), (x1, y1))


def step_kernel(
    n_gx, n_gy, counts, links_in, maps_in, conv_in, down_in, head_in, features, grad_in,
    latent, out, total,
    links, maps, conv, down, head, blocks, grad_own, grad_far, table, tables, down_rows, turned, pool, tall, taps, slope,
    act, octants, received, inverse, hidden_grad, planes, near, far_out, far_in, conv_acc, down_acc,
    head_acc, final_taps, coarse,
    grads, part_1, part_2, part_3,
    known, load_s, face_s, face_r, merge_s, merge_r, back_s, back_r, ret_s, ret_r,
    send_1, recv_1, send_2, recv_2, send_3, recv_3,
):
    nz = ring_z(n_gx)
    ny, nc = n_gx // nz, n_gy // 2
    plane_size = nc * ny
    x, me = lax.axis_index("gx"), lax.axis_index("gy")
    y, z = lax.div(x, nz), lax.rem(x, nz)
    chip, core = lax.div(me, 2), lax.rem(me, 2)
    spot = chip * ny + y
    beside = around(n_gx, n_gy)
    merged = partners()
    mate = merged[1]
    rows_z = [(y * nz + lax.rem(z + k, nz), me) for k in range(1, nz)]
    flat = []
    for k in range(1, 2 * plane_size):
        near_by = k % plane_size
        across_c, across_y = near_by // ny, near_by % ny
        other_c = lax.rem(chip + across_c, nc)
        other_y = lax.rem(y + across_y, ny)
        other = core if k < plane_size else 1 - core
        far_off = min(across_c, nc - across_c) + min(across_y, ny - across_y)
        device = (other_y * nz + z, other_c * 2 + other)
        flat.append((far_off, k, device, other, other_c * ny + other_y))
    flat.sort(key=lambda entry: -entry[0])
    order_z = sorted(range(1, nz), key=lambda k: -min(k, nz - k))
    ring = [
        (y * nz + lax.rem(z + 1, nz), me), (y * nz + lax.rem(z + nz - 1, nz), me),
        (lax.rem(y + 1, ny) * nz + z, me), (lax.rem(y + ny - 1, ny) * nz + z, me),
        (x, lax.rem(chip + 1, nc) * 2 + core), (x, lax.rem(chip + nc - 1, nc) * 2 + core), mate,
    ]
    everyone = list(beside) + list(merged) + ring

    def tell(number):
        for device in ring:
            pl.semaphore_signal(known.at[number], inc=1, device_id=device, device_id_type=MESH)

    def hear(number):
        pl.semaphore_wait(known.at[number], len(ring))

    rim = edges(n_gx, n_gy)
    low_half = lanes() < 64
    zero = jnp.zeros((64, 128), BF16)

    def send(source, target, sends, recvs, k, device):
        return pltpu.make_async_remote_copy(
            src_ref=source, dst_ref=target, send_sem=sends.at[k[0]], recv_sem=recvs.at[k[1]],
            device_id=device, device_id_type=MESH,
        )

    def whole(like, sends, recvs, k):
        return send(like, like, sends, recvs, k, mate)

    barrier = pltpu.get_barrier_semaphore()
    for device in everyone:
        pl.semaphore_signal(barrier, inc=1, device_id=device, device_id_type=MESH)

    def load(i):
        return pltpu.make_async_copy(
            features.at[pl.ds(2 * i, 2)], blocks.at[pl.ds(2 * i, 2)], load_s.at[i]
        )

    for i in range(4):
        load(i).start()
    table_loads = [
        pltpu.make_async_copy(maps_in, maps, load_s.at[8]),
        pltpu.make_async_copy(links_in, links, load_s.at[9]),
    ]
    for copy in table_loads:
        copy.start()
    grad_load = pltpu.make_async_copy(grad_in, grad_own, load_s.at[4])
    grad_load.start()
    weight_loads = [
        pltpu.make_async_copy(source, target, load_s.at[5 + k])
        for k, (source, target) in enumerate(((down_in, down), (conv_in, conv), (head_in, head)))
    ]
    for copy in weight_loads:
        copy.start()
    for d in range(4):
        pool[d, 8] = zero
    for d in range(2):
        for j in range(4, 9):
            tall[d, j] = zero
    def pack(i, carry):
        load(i).wait()
        keep_a = flag(counts[0] - 2 * i) > 0
        keep_b = flag(counts[0] - 2 * i) > 1
        cols = [None] * 8
        for pq in range(4):
            a = jnp.where(keep_a, blocks[2 * i, :, pq * 128 : pq * 128 + 128], zero)
            b = jnp.where(keep_b, blocks[2 * i + 1, :, pq * 128 : pq * 128 + 128], zero)
            cols[2 * pq] = jnp.where(low_half, a, roll(b, 64))
            cols[2 * pq + 1] = jnp.where(low_half, roll(a, 64), b)
        for d in range(6):
            rows = pool.at[d, i] if d < 4 else tall.at[d - 4, i]
            rows[...] = pack_face(cols, d // 2, d % 2 == 0)
        for c in range(8):
            taps[i, 0:64, c * 128 : c * 128 + 128] = cols[c]
        return carry

    lax.fori_loop(0, 4, pack, 0, unroll=True)
    for copy in table_loads:
        copy.wait()
    lane = lax.broadcasted_iota(jnp.int32, (8, 128), 1)
    values = jnp.full((8, 128), -1, jnp.int32)
    for k in range(8):
        values = jnp.where(lane == k, jnp.broadcast_to(maps[0, k], (8, 128)), values)
    table[...] = values
    for copy in weight_loads:
        copy.wait()
    down_rows[...] = dot(selection(), down[...], 1, 1).astype(BF16)
    grad_load.wait()
    pl.semaphore_wait(barrier, len(everyone))
    tell(0)
    face_copies = [
        send(pool.at[d, pl.ds(0, 4)], pool.at[d, pl.ds(4, 4)], face_s, face_r, (0, 0), beside[d])
        for d in range(4)
    ] + [send(table, tables.at[m], face_s, face_r, (1, 1), merged[m]) for m in range(3)]
    for copy in face_copies:
        copy.start()

    def grad_chunk(i):
        return send(
            grad_own.at[pl.ds(2 * i, 2)], grad_far.at[pl.ds(2 * i, 2)], back_s, back_r,
            (0, i), merged[0],
        )

    def grad_relay(i):
        return send(
            grad_far.at[pl.ds(2 * i, 2)], grad_far.at[pl.ds(16 + 2 * i, 2)], back_s, back_r,
            (2, 5), mate,
        )

    grad_mate = send(grad_own, grad_far.at[pl.ds(8, 8)], back_s, back_r, (1, 4), mate)
    octant_far = send(octants, received.at[pl.ds(0, 8)], merge_s, merge_r, (0, 0), merged[0])
    octant_mate = send(octants, received.at[pl.ds(8, 8)], merge_s, merge_r, (1, 1), mate)
    octant_relay = send(
        received.at[pl.ds(0, 8)], received.at[pl.ds(16, 8)], merge_s, merge_r, (2, 2), mate
    )
    for i in range(4):
        grad_chunk(i).start()
    grad_mate.start()

    def tap(i, d):
        cols = [taps[i, 0:64, c * 128 : c * 128 + 128] for c in range(8)]
        e0 = link_of(links, 2 * i, d, rim)
        e1 = link_of(links, 2 * i + 1, d, rim)
        rows = pool.at[d] if d < 4 else tall.at[d - 4]
        face = jnp.where(
            low_half,
            pltpu.roll(rows[lax.div(e0, 2)], 64 * lax.rem(e0, 2), 1),
            pltpu.roll(rows[lax.div(e1, 2)], 64 - 64 * lax.rem(e1, 2), 1),
        )
        moved = (shift_minus if d % 2 == 0 else shift_plus)(cols, d // 2, face)
        for c in range(8):
            taps[i, 64 * (d + 1) : 64 * (d + 2), c * 128 : c * 128 + 128] = moved[c]

    def upright(i, carry):
        tap(i, 4)
        tap(i, 5)
        return carry

    lax.fori_loop(0, 4, upright, 0, unroll=True)
    for d in range(7):
        block = conv[:, d * 64 : d * 64 + 64].astype(F32)
        turned[:, d * 64 : d * 64 + 64] = block.T.astype(BF16)
    conv_acc[...] = jnp.zeros_like(conv_acc)
    down_acc[...] = jnp.zeros_like(down_acc)
    head_acc[...] = jnp.zeros_like(head_acc)
    whole(far_in, face_s, face_r, (0, 0)).wait()
    whole(tables, face_s, face_r, (1, 1)).wait()
    hear(0)
    tell(1)

    def level(i, carry):
        for d in range(4):
            tap(i, d)
        values = dot(conv[...], taps[i], 1, 0)
        s = sigmoid(values)
        slope[i] = s * (1.0 + values * (1.0 - s))
        active = (values * s).astype(BF16)
        for c in range(8):
            act[i, c * 64 : c * 64 + 64, :] = active[:, c * 128 : c * 128 + 128]
        rows = dot(act[i], down_rows[...], 0, 0).astype(BF16)
        octants[2 * i] = rows[:64]
        octants[2 * i + 1] = rows[64:]
        grad_chunk(i).wait_recv()
        grad_relay(i).start()
        return carry

    lax.fori_loop(0, 4, level, 0, unroll=True)
    for s in range(8):
        found = jnp.zeros((8, 128), jnp.int32)
        for m in range(4):
            entries = table[...] if m == 0 else tables[m - 1]
            found = jnp.where(entries == m * 8 + s, m * 8 + lane - 32, found)
        inverse[s] = jnp.clip(jnp.sum(found[0:1, :]) + 32, 0, 32)

    hear(1)
    tell(2)
    whole(grad_own, back_s, back_r, (0, 0)).wait_send()
    grad_mate.wait()
    whole(grad_own, back_s, back_r, (2, 5)).wait()

    def merged_row(e, own, other):
        mine = own[jnp.clip(e, 0, 7)]
        theirs = other[jnp.clip(e - 8, 0, 23)]
        return jnp.where(flag(e) < 8, mine, jnp.where(flag(e) < 32, theirs, zero))

    def backward(i, carry):
        named = jnp.concatenate([
            merged_row(inverse[2 * i], grad_own, grad_far),
            merged_row(inverse[2 * i + 1], grad_own, grad_far),
        ], axis=0)
        values = jnp.concatenate([octants[2 * i], octants[2 * i + 1]], axis=0).astype(F32)
        s = sigmoid(values)
        active = (values * s).astype(BF16)
        head_acc[...] += dot(named, active, 0, 0)
        rows = dot(named, head[...], 1, 0) * (s * (1.0 + values * (1.0 - s)))
        rows = rows.astype(BF16)
        down_acc[...] += dot(act[i], rows, 1, 0)
        patch = dot(down_rows[...], rows, 1, 1)
        for c in range(8):
            factor = slope[i, :, c * 128 : c * 128 + 128]
            value = (patch[c * 64 : c * 64 + 64] * factor).astype(BF16)
            hidden_grad[i, :, c * 128 : c * 128 + 128] = value
        conv_acc[...] += dot(hidden_grad[i], taps[i], 1, 1)
        return carry

    lax.fori_loop(0, 4, backward, 0, unroll=True)
    per = GRAD_ROWS // 2 // plane_size

    def put(row, values):
        half, first = row // (GRAD_ROWS // 2), row % (GRAD_ROWS // 2) // per
        count = values.shape[0] // per
        grads[half, first : first + count] = values.reshape(count, per, 128)

    wide = conv_acc[...].astype(BF16)
    for j in range(3):
        put(j * 64, wide[:, j * 128 : j * 128 + 128])
    put(192, jnp.concatenate([wide[:, 384:448], jnp.zeros((64, 64), BF16)], axis=1))
    ordered = dot(down_acc[...].astype(BF16), selection(), 0, 0).astype(BF16)
    for j in range(4):
        put(256 + 128 * j, ordered[:, j * 128 : j * 128 + 128])
    put(768, head_acc[...].astype(BF16))
    put(896, jnp.zeros((128, 128), BF16))
    hear(2)
    tell(3)
    copies_1 = [
        send(grads.at[half, place], part_1.at[k], send_1, recv_1, (0, 0), device)
        for _, k, device, half, place in flat
    ]
    for copy in copies_1:
        copy.start()
    octant_far.start()
    octant_mate.start()

    def plane(i, carry):
        cols = [hidden_grad[i, :, c * 128 : c * 128 + 128] for c in range(8)]
        for d in range(6):
            face = pack_face(cols, d // 2, d % 2 == 1)
            planes[d, 0, i] = face.astype(F32)
            planes[d, 1, i] = roll(face, 64).astype(F32)
        return carry

    def gathered(d, j):
        out = jnp.zeros((64, 128), F32)
        for i in range(4):
            e0 = link_of(links, 2 * i, d, rim)
            e1 = link_of(links, 2 * i + 1, d, rim)
            straight = jnp.where(low_half, flag(e0), flag(e1 - 1))
            crossed = jnp.where(low_half, flag(e1), flag(e0 - 1))
            out = out + jnp.where(straight == 2 * j, planes[d, 0, i], 0.0)
            out = out + jnp.where(crossed == 2 * j, planes[d, 1, i], 0.0)
        return out

    def collect_far(j, carry):
        for d in range(4):
            far_out[d, j] = gathered(d, 4 + j).astype(BF16)
        return carry

    def collect_near(j, carry):
        for d in range(6):
            near[d, j] = gathered(d, j)
        return carry

    lax.fori_loop(0, 4, plane, 0)
    lax.fori_loop(0, 4, collect_far, 0)
    target = (beside[1], beside[0], beside[3], beside[2])
    returns = [send(far_out.at[d], far_in.at[d], ret_s, ret_r, (0, 0), target[d]) for d in range(4)]
    for copy in returns:
        copy.start()
    others = part_1.at[pl.ds(1, 2 * plane_size - 1)]
    whole(others, send_1, recv_1, (0, 0)).wait()
    result = grads[core, spot].astype(F32)
    for k in range(1, 2 * plane_size):
        result = result + part_1[k].astype(F32)
    part_2[z] = result.astype(BF16)
    copies_2 = [
        send(part_2.at[z], part_2.at[z], send_2, recv_2, (0, 0), rows_z[k - 1]) for k in order_z
    ]
    for copy in copies_2:
        copy.start()
    octant_far.wait_recv()
    octant_relay.start()
    lax.fori_loop(0, 4, collect_near, 0)
    whole(far_in, ret_s, ret_r, (0, 0)).wait()

    def final(i, carry):
        cols = [hidden_grad[i, :, c * 128 : c * 128 + 128] for c in range(8)]
        for c in range(8):
            final_taps[0:64, c * 128 : c * 128 + 128] = cols[c]
        for d in range(6):
            face = near[d, i]
            if d < 4:
                face = face + far_in[d, i].astype(F32)
            moved = (shift_plus if d % 2 == 0 else shift_minus)(cols, d // 2, face.astype(BF16))
            for c in range(8):
                final_taps[64 * (d + 1) : 64 * (d + 2), c * 128 : c * 128 + 128] = moved[c]
        values = dot(turned[...], final_taps[...], 1, 0)
        keep_a = flag(counts[0] - 2 * i) > 0
        keep_b = flag(counts[0] - 2 * i) > 1
        for pq in range(4):
            even = values[:, pq * 256 : pq * 256 + 128]
            odd = values[:, pq * 256 + 128 : pq * 256 + 256]
            a = jnp.where(low_half, even, roll(odd, 64))
            b = jnp.where(low_half, roll(even, 64), odd)
            spread = slice(pq * 128, pq * 128 + 128)
            out[2 * i, :, spread] = jnp.where(keep_a, a, 0.0).astype(BF16)
            out[2 * i + 1, :, spread] = jnp.where(keep_b, b, 0.0).astype(BF16)
        return carry

    lax.fori_loop(0, 4, final, 0, unroll=True)
    whole(part_2.at[pl.ds(0, nz - 1)], send_2, recv_2, (0, 0)).wait()
    result = part_2[0].astype(F32)
    for k in range(1, nz):
        result = result + part_2[k].astype(F32)
    part_3[...] = result.astype(BF16)
    hear(3)
    copies_3 = [
        send(part_3, total.at[core, spot], send_3, recv_3, (0, 0), device)
        for _, _, device, _, _ in flat
    ]
    for copy in copies_3:
        copy.start()
    total[core, spot] = result.astype(BF16)
    octant_far.wait_send()
    octant_mate.wait()
    octant_relay.wait()
    for k in range(8):
        coarse[k * 64 : k * 64 + 64, :] = merged_row(maps[0, k], octants, received)
    values = coarse[...].astype(F32)
    active = (values * sigmoid(values)).astype(BF16)
    latent[...] = dot(active, head[...], 1, 1).astype(BF16)
    whole(others, send_3, recv_3, (0, 0)).wait()


def unpack_kernel(
    latent, features, total, latent_out, features_out, conv_out, down_out, head_out,
    conv_hold, down_hold, head_hold, store_s,
):
    scale = float(2048) ** -0.5
    moves = [(features, features_out), (latent, latent_out.at[0])]
    moves += [(conv_hold, conv_out), (down_hold, down_out), (head_hold, head_out)]
    stores = [
        pltpu.make_async_copy(source, target, store_s.at[k])
        for k, (source, target) in enumerate(moves)
    ]
    stores[0].start()
    stores[1].start()
    rows = total[...].reshape(GRAD_ROWS, 128)

    def scaled(first, last):
        return rows[first:last].astype(F32) * scale

    for j in range(4):
        down_hold[:, j * 128 : j * 128 + 128] = scaled(256 + j * 128, 384 + j * 128)
    stores[3].start()
    for j in range(3):
        conv_hold[:, j * 128 : j * 128 + 128] = scaled(j * 64, j * 64 + 64)
    conv_hold[:, 384:448] = scaled(192, 256)[:, :64]
    stores[2].start()
    head_hold[...] = scaled(768, 896)
    stores[4].start()
    for store in stores:
        store.wait()


VM = pl.BlockSpec(memory_space=pltpu.VMEM)
SM = pl.BlockSpec(memory_space=pltpu.SMEM)
ANY = pl.BlockSpec(memory_space=pl.ANY)
HBM = pl.BlockSpec(memory_space=pltpu.HBM)
DMA = pltpu.SemaphoreType.DMA
VMEM = pltpu.VMEM


def shape(*dims, dtype=BF16):
    return jax.ShapeDtypeStruct(dims, dtype)


def bind(kernel, *fixed):
    def run(*refs):
        kernel(*fixed, *refs)

    return run


def body(
    features, neighbours, counts, conv_weight, down_weight, head_weight, coarse_map, latent_grad
):
    n_gx, n_gy = lax.axis_size("gx"), lax.axis_size("gy")
    nz = ring_z(n_gx)
    spots = (n_gx // nz) * (n_gy // 2)
    per = GRAD_ROWS // 2 // spots
    latent, grad, total = pl.pallas_call(
        bind(step_kernel, n_gx, n_gy), name="step", in_specs=[SM] + [HBM] * 7,
        out_specs=[VM] * 3,
        out_shape=[shape(512, 128), shape(8, 64, 512), shape(2, spots, per, 128)],
        scratch_shapes=[
            pltpu.SMEM((8, 6), jnp.int32), pltpu.SMEM((1, 8), jnp.int32),
            VMEM((64, 448), BF16), VMEM((128, 512), BF16), VMEM((128, 128), BF16),
            VMEM((8, 64, 512), BF16), VMEM((8, 64, 128), BF16), VMEM((24, 64, 128), BF16),
            VMEM((8, 128), jnp.int32), VMEM((3, 8, 128), jnp.int32),
            VMEM((512, 128), BF16), VMEM((64, 448), BF16), VMEM((4, 9, 64, 128), BF16), VMEM((2, 9, 64, 128), BF16),
            VMEM((4, 448, 1024), BF16), VMEM((4, 64, 1024), F32), VMEM((4, 512, 128), BF16),
            VMEM((8, 64, 128), BF16), VMEM((24, 64, 128), BF16),
            pltpu.SMEM((8,), jnp.int32), VMEM((4, 64, 1024), BF16), VMEM((6, 2, 4, 64, 128), F32),
            VMEM((6, 4, 64, 128), F32), VMEM((4, 4, 64, 128), BF16), VMEM((4, 4, 64, 128), BF16),
            VMEM((64, 448), F32), VMEM((512, 128), F32), VMEM((128, 128), F32),
            VMEM((448, 1024), BF16), VMEM((512, 128), BF16),
            VMEM((2, spots, per, 128), BF16), VMEM((2 * spots, per, 128), BF16),
            VMEM((nz, per, 128), BF16), VMEM((per, 128), BF16),
            pltpu.SemaphoreType.REGULAR((4,)), DMA((10,)),
            DMA((2,)), DMA((2,)), DMA((3,)), DMA((3,)), DMA((3,)), DMA((6,)),
            DMA((1,)), DMA((1,)), DMA((1,)), DMA((1,)), DMA((1,)), DMA((1,)), DMA((1,)), DMA((1,)),
        ],
        compiler_params=pltpu.CompilerParams(
            collective_id=0, has_side_effects=True, vmem_limit_bytes=20 * 2**20
        ),
    )(
        counts, *[
            pltpu.with_memory_space_constraint(value, pltpu.HBM)
            for value in (
                neighbours, coarse_map, conv_weight, down_weight, head_weight, features,
                latent_grad.reshape(8, 64, 128),
            )
        ],
    )
    return pl.pallas_call(
        unpack_kernel, name="unpack", in_specs=[VM] * 3, out_specs=[ANY] * 5,
        out_shape=[
            shape(1, 512, 128), shape(8, 64, 512), shape(64, 448, dtype=F32),
            shape(128, 512, dtype=F32), shape(128, 128, dtype=F32),
        ],
        scratch_shapes=[
            VMEM((64, 448), F32), VMEM((128, 512), F32), VMEM((128, 128), F32), DMA((5,)),
        ],
        compiler_params=pltpu.CompilerParams(vmem_limit_bytes=8 * 2**20),
    )(latent, grad, total)


def solution(mesh):
    placed = (
        P(("gx", "gy"), None, None),
        P(("gx", "gy"), None),
        P(("gx", "gy")),
        P(),
        P(),
        P(),
        P(("gx", "gy"), None),
        P(("gx", "gy"), None, None),
    )
    return jax.shard_map(
        body,
        mesh=mesh,
        in_specs=placed,
        out_specs=(P(("gx", "gy"), None, None), P(("gx", "gy"), None, None), P(), P(), P()),
        check_vma=False,
    )
```

```python
import jax
import jax.numpy as jnp
from jax import lax
from jax.experimental import pallas as pl
from jax.experimental.pallas import tpu as pltpu
from jax.sharding import PartitionSpec as P

MESH = pl.DeviceIdType.MESH
F32 = jnp.float32
BF16 = jnp.bfloat16
STRIDE = (16, 4, 1)
GRAD_ROWS = 1024


def ring_z(n_gx):
    return 8 if n_gx % 8 == 0 else n_gx // 2


def dot(a, b, ca, cb):
    return lax.dot_general(a, b, (((ca,), (cb,)), ((), ())), preferred_element_type=F32)


def lanes():
    return lax.broadcasted_iota(jnp.int32, (64, 128), 1)


def flag(value):
    return jnp.broadcast_to(value, (64, 128))


def roll(values, amount):
    amount = amount % 128
    return values if amount == 0 else pltpu.roll(values, amount, 1)


def column(axis, bit, s):
    high, low = s // 2, s % 2
    bits = [high, low]
    bits.insert(axis, bit)
    return bits[0] * 4 + bits[1] * 2 + bits[2]


def field(axis):
    return lax.rem(lax.div(lanes(), STRIDE[axis]), 4)


def pack_face(cols, axis, upper):
    step = STRIDE[axis]
    place = field(axis)
    out = None
    for s in range(4):
        shift = step * (s - 3) if upper else step * s
        moved = roll(cols[column(axis, int(upper), s)], shift)
        out = moved if out is None else jnp.where(place == s, moved, out)
    return out


def shift_minus(cols, axis, face):
    step = STRIDE[axis]
    edge = field(axis) == 0
    out = [None] * 8
    for s in range(4):
        low, high = column(axis, 0, s), column(axis, 1, s)
        out[high] = cols[low]
        out[low] = jnp.where(edge, roll(face, -step * s), roll(cols[high], step))
    return out


def shift_plus(cols, axis, face):
    step = STRIDE[axis]
    edge = field(axis) == 3
    out = [None] * 8
    for s in range(4):
        low, high = column(axis, 0, s), column(axis, 1, s)
        out[low] = cols[high]
        out[high] = jnp.where(edge, roll(face, step * (3 - s)), roll(cols[low], -step))
    return out


def sigmoid(values):
    return 1.0 / (1.0 + jnp.exp(-values))


def edges(n_gx, n_gy):
    x, y = lax.axis_index("gx"), lax.axis_index("gy")
    return (x == 0, x == n_gx - 1, y == 0, y == n_gy - 1)


def link_of(links, slot, direction, rim):
    value = links[slot, direction]
    if direction < 4:
        return jnp.where(jnp.logical_and(rim[direction], value >= 8), 16, value)
    return value


def selection():
    row = lax.broadcasted_iota(jnp.int32, (512, 512), 0)
    col = lax.broadcasted_iota(jnp.int32, (512, 512), 1)
    return jnp.where(col == lax.rem(row, 64) * 8 + lax.div(row, 64), 1.0, 0.0).astype(BF16)


def around(n_gx, n_gy):
    x, y = lax.axis_index("gx"), lax.axis_index("gy")
    return (
        (lax.rem(x + 1, n_gx), y),
        (lax.rem(x + n_gx - 1, n_gx), y),
        (x, lax.rem(y + 1, n_gy)),
        (x, lax.rem(y + n_gy - 1, n_gy)),
    )


def partners():
    x, y = lax.axis_index("gx"), lax.axis_index("gy")
    x1 = x + 1 - 2 * lax.rem(x, 2)
    y1 = y + 1 - 2 * lax.rem(y, 2)
    return ((x1, y), (x, y1), (x1, y1))


def step_kernel(
    n_gx, n_gy, counts, links_in, maps_in, conv_in, down_in, head_in, features, grad_in,
    latent, out, total,
    links, maps, conv, down, head, blocks, grad_own, grad_far, table, tables, down_rows, turned, pool, tall, taps, slope,
    act, octants, received, inverse, hidden_grad, planes, near, far_out, far_in, conv_acc, down_acc,
    head_acc, final_taps, coarse,
    grads, part_1, part_2, part_3,
    known, load_s, face_s, face_r, merge_s, merge_r, back_s, back_r, ret_s, ret_r,
    send_1, recv_1, send_2, recv_2, send_3, recv_3,
):
    nz = ring_z(n_gx)
    ny, nc = n_gx // nz, n_gy // 2
    plane_size = nc * ny
    x, me = lax.axis_index("gx"), lax.axis_index("gy")
    y, z = lax.div(x, nz), lax.rem(x, nz)
    chip, core = lax.div(me, 2), lax.rem(me, 2)
    spot = chip * ny + y
    beside = around(n_gx, n_gy)
    merged = partners()
    mate = merged[1]
    rows_z = [(y * nz + lax.rem(z + k, nz), me) for k in range(1, nz)]
    flat = []
    for k in range(1, 2 * plane_size):
        near_by = k % plane_size
        across_c, across_y = near_by // ny, near_by % ny
        other_c = lax.rem(chip + across_c, nc)
        other_y = lax.rem(y + across_y, ny)
        other = core if k < plane_size else 1 - core
        far_off = min(across_c, nc - across_c) + min(across_y, ny - across_y)
        device = (other_y * nz + z, other_c * 2 + other)
        flat.append((far_off, k, device, other, other_c * ny + other_y))
    flat.sort(key=lambda entry: -entry[0])
    order_z = sorted(range(1, nz), key=lambda k: -min(k, nz - k))
    ring = [
        (y * nz + lax.rem(z + 1, nz), me), (y * nz + lax.rem(z + nz - 1, nz), me),
        (lax.rem(y + 1, ny) * nz + z, me), (lax.rem(y + ny - 1, ny) * nz + z, me),
        (x, lax.rem(chip + 1, nc) * 2 + core), (x, lax.rem(chip + nc - 1, nc) * 2 + core), mate,
    ]
    everyone = list(beside) + list(merged) + ring

    def tell(number):
        for device in ring:
            pl.semaphore_signal(known.at[number], inc=1, device_id=device, device_id_type=MESH)

    def hear(number):
        pl.semaphore_wait(known.at[number], len(ring))

    rim = edges(n_gx, n_gy)
    low_half = lanes() < 64
    zero = jnp.zeros((64, 128), BF16)

    def send(source, target, sends, recvs, k, device):
        return pltpu.make_async_remote_copy(
            src_ref=source, dst_ref=target, send_sem=sends.at[k[0]], recv_sem=recvs.at[k[1]],
            device_id=device, device_id_type=MESH,
        )

    def whole(like, sends, recvs, k):
        return send(like, like, sends, recvs, k, mate)

    barrier = pltpu.get_barrier_semaphore()
    for device in everyone:
        pl.semaphore_signal(barrier, inc=1, device_id=device, device_id_type=MESH)

    def load(i):
        return pltpu.make_async_copy(
            features.at[pl.ds(2 * i, 2)], blocks.at[pl.ds(2 * i, 2)], load_s.at[i]
        )

    for i in range(4):
        load(i).start()
    table_loads = [
        pltpu.make_async_copy(maps_in, maps, load_s.at[8]),
        pltpu.make_async_copy(links_in, links, load_s.at[9]),
    ]
    for copy in table_loads:
        copy.start()
    grad_load = pltpu.make_async_copy(grad_in, grad_own, load_s.at[4])
    grad_load.start()
    weight_loads = [
        pltpu.make_async_copy(source, target, load_s.at[5 + k])
        for k, (source, target) in enumerate(((down_in, down), (conv_in, conv), (head_in, head)))
    ]
    for copy in weight_loads:
        copy.start()
    for d in range(4):
        pool[d, 8] = zero
    for d in range(2):
        for j in range(4, 9):
            tall[d, j] = zero
    def pack(i, carry):
        load(i).wait()
        keep_a = flag(counts[0] - 2 * i) > 0
        keep_b = flag(counts[0] - 2 * i) > 1
        cols = [None] * 8
        for pq in range(4):
            a = jnp.where(keep_a, blocks[2 * i, :, pq * 128 : pq * 128 + 128], zero)
            b = jnp.where(keep_b, blocks[2 * i + 1, :, pq * 128 : pq * 128 + 128], zero)
            cols[2 * pq] = jnp.where(low_half, a, roll(b, 64))
            cols[2 * pq + 1] = jnp.where(low_half, roll(a, 64), b)
        for d in range(6):
            rows = pool.at[d, i] if d < 4 else tall.at[d - 4, i]
            rows[...] = pack_face(cols, d // 2, d % 2 == 0)
        for c in range(8):
            taps[i, 0:64, c * 128 : c * 128 + 128] = cols[c]
        return carry

    lax.fori_loop(0, 4, pack, 0, unroll=True)
    for copy in table_loads:
        copy.wait()
    lane = lax.broadcasted_iota(jnp.int32, (8, 128), 1)
    values = jnp.full((8, 128), -1, jnp.int32)
    for k in range(8):
        values = jnp.where(lane == k, jnp.broadcast_to(maps[0, k], (8, 128)), values)
    table[...] = values
    pl.semaphore_wait(barrier, len(everyone))
    tell(0)
    face_copies = [
        send(pool.at[d, pl.ds(0, 4)], pool.at[d, pl.ds(4, 4)], face_s, face_r, (0, 0), beside[d])
        for d in range(4)
    ] + [send(table, tables.at[m], face_s, face_r, (1, 1), merged[m]) for m in range(3)]
    for copy in face_copies:
        copy.start()

    def grad_chunk(i):
        return send(
            grad_own.at[pl.ds(2 * i, 2)], grad_far.at[pl.ds(2 * i, 2)], back_s, back_r,
            (0, i), merged[0],
        )

    def grad_relay(i):
        return send(
            grad_far.at[pl.ds(2 * i, 2)], grad_far.at[pl.ds(16 + 2 * i, 2)], back_s, back_r,
            (2, 5), mate,
        )

    grad_mate = send(grad_own, grad_far.at[pl.ds(8, 8)], back_s, back_r, (1, 4), mate)
    octant_far = send(octants, received.at[pl.ds(0, 8)], merge_s, merge_r, (0, 0), merged[0])
    octant_mate = send(octants, received.at[pl.ds(8, 8)], merge_s, merge_r, (1, 1), mate)
    octant_relay = send(
        received.at[pl.ds(0, 8)], received.at[pl.ds(16, 8)], merge_s, merge_r, (2, 2), mate
    )
    grad_load.wait()
    for i in range(4):
        grad_chunk(i).start()
    grad_mate.start()
    for copy in weight_loads:
        copy.wait()
    down_rows[...] = dot(selection(), down[...], 1, 1).astype(BF16)

    def tap(i, d):
        cols = [taps[i, 0:64, c * 128 : c * 128 + 128] for c in range(8)]
        e0 = link_of(links, 2 * i, d, rim)
        e1 = link_of(links, 2 * i + 1, d, rim)
        rows = pool.at[d] if d < 4 else tall.at[d - 4]
        face = jnp.where(
            low_half,
            pltpu.roll(rows[lax.div(e0, 2)], 64 * lax.rem(e0, 2), 1),
            pltpu.roll(rows[lax.div(e1, 2)], 64 - 64 * lax.rem(e1, 2), 1),
        )
        moved = (shift_minus if d % 2 == 0 else shift_plus)(cols, d // 2, face)
        for c in range(8):
            taps[i, 64 * (d + 1) : 64 * (d + 2), c * 128 : c * 128 + 128] = moved[c]

    def upright(i, carry):
        tap(i, 4)
        tap(i, 5)
        return carry

    lax.fori_loop(0, 4, upright, 0, unroll=True)
    for d in range(7):
        block = conv[:, d * 64 : d * 64 + 64].astype(F32)
        turned[:, d * 64 : d * 64 + 64] = block.T.astype(BF16)
    conv_acc[...] = jnp.zeros_like(conv_acc)
    down_acc[...] = jnp.zeros_like(down_acc)
    head_acc[...] = jnp.zeros_like(head_acc)
    whole(far_in, face_s, face_r, (0, 0)).wait()
    whole(tables, face_s, face_r, (1, 1)).wait()
    hear(0)
    tell(1)

    def level(i, carry):
        for d in range(4):
            tap(i, d)
        values = dot(conv[...], taps[i], 1, 0)
        s = sigmoid(values)
        slope[i] = s * (1.0 + values * (1.0 - s))
        active = (values * s).astype(BF16)
        for c in range(8):
            act[i, c * 64 : c * 64 + 64, :] = active[:, c * 128 : c * 128 + 128]
        rows = dot(act[i], down_rows[...], 0, 0).astype(BF16)
        octants[2 * i] = rows[:64]
        octants[2 * i + 1] = rows[64:]
        grad_chunk(i).wait_recv()
        grad_relay(i).start()
        return carry

    lax.fori_loop(0, 4, level, 0, unroll=True)
    for s in range(8):
        found = jnp.zeros((8, 128), jnp.int32)
        for m in range(4):
            entries = table[...] if m == 0 else tables[m - 1]
            found = jnp.where(entries == m * 8 + s, m * 8 + lane - 32, found)
        inverse[s] = jnp.clip(jnp.sum(found[0:1, :]) + 32, 0, 32)

    hear(1)
    tell(2)
    whole(grad_own, back_s, back_r, (0, 0)).wait_send()
    grad_mate.wait()
    whole(grad_own, back_s, back_r, (2, 5)).wait()

    def merged_row(e, own, other):
        mine = own[jnp.clip(e, 0, 7)]
        theirs = other[jnp.clip(e - 8, 0, 23)]
        return jnp.where(flag(e) < 8, mine, jnp.where(flag(e) < 32, theirs, zero))

    def backward(i, carry):
        named = jnp.concatenate([
            merged_row(inverse[2 * i], grad_own, grad_far),
            merged_row(inverse[2 * i + 1], grad_own, grad_far),
        ], axis=0)
        values = jnp.concatenate([octants[2 * i], octants[2 * i + 1]], axis=0).astype(F32)
        s = sigmoid(values)
        active = (values * s).astype(BF16)
        head_acc[...] += dot(named, active, 0, 0)
        rows = dot(named, head[...], 1, 0) * (s * (1.0 + values * (1.0 - s)))
        rows = rows.astype(BF16)
        down_acc[...] += dot(act[i], rows, 1, 0)
        patch = dot(down_rows[...], rows, 1, 1)
        for c in range(8):
            factor = slope[i, :, c * 128 : c * 128 + 128]
            value = (patch[c * 64 : c * 64 + 64] * factor).astype(BF16)
            hidden_grad[i, :, c * 128 : c * 128 + 128] = value
        conv_acc[...] += dot(hidden_grad[i], taps[i], 1, 1)
        return carry

    lax.fori_loop(0, 4, backward, 0, unroll=True)
    per = GRAD_ROWS // 2 // plane_size

    def put(row, values):
        half, first = row // (GRAD_ROWS // 2), row % (GRAD_ROWS // 2) // per
        count = values.shape[0] // per
        grads[half, first : first + count] = values.reshape(count, per, 128)

    wide = conv_acc[...].astype(BF16)
    for j in range(3):
        put(j * 64, wide[:, j * 128 : j * 128 + 128])
    put(192, jnp.concatenate([wide[:, 384:448], jnp.zeros((64, 64), BF16)], axis=1))
    ordered = dot(down_acc[...].astype(BF16), selection(), 0, 0).astype(BF16)
    for j in range(4):
        put(256 + 128 * j, ordered[:, j * 128 : j * 128 + 128])
    put(768, head_acc[...].astype(BF16))
    put(896, jnp.zeros((128, 128), BF16))
    hear(2)
    tell(3)
    copies_1 = [
        send(grads.at[half, place], part_1.at[k], send_1, recv_1, (0, 0), device)
        for _, k, device, half, place in flat
    ]
    for copy in copies_1:
        copy.start()
    octant_far.start()
    octant_mate.start()

    def plane(i, carry):
        cols = [hidden_grad[i, :, c * 128 : c * 128 + 128] for c in range(8)]
        for d in range(6):
            face = pack_face(cols, d // 2, d % 2 == 1)
            planes[d, 0, i] = face.astype(F32)
            planes[d, 1, i] = roll(face, 64).astype(F32)
        return carry

    def gathered(d, j):
        out = jnp.zeros((64, 128), F32)
        for i in range(4):
            e0 = link_of(links, 2 * i, d, rim)
            e1 = link_of(links, 2 * i + 1, d, rim)
            straight = jnp.where(low_half, flag(e0), flag(e1 - 1))
            crossed = jnp.where(low_half, flag(e1), flag(e0 - 1))
            out = out + jnp.where(straight == 2 * j, planes[d, 0, i], 0.0)
            out = out + jnp.where(crossed == 2 * j, planes[d, 1, i], 0.0)
        return out

    def collect_far(j, carry):
        for d in range(4):
            far_out[d, j] = gathered(d, 4 + j).astype(BF16)
        return carry

    def collect_near(j, carry):
        for d in range(6):
            near[d, j] = gathered(d, j)
        return carry

    lax.fori_loop(0, 4, plane, 0)
    lax.fori_loop(0, 4, collect_far, 0)
    target = (beside[1], beside[0], beside[3], beside[2])
    returns = [send(far_out.at[d], far_in.at[d], ret_s, ret_r, (0, 0), target[d]) for d in range(4)]
    for copy in returns:
        copy.start()
    others = part_1.at[pl.ds(1, 2 * plane_size - 1)]
    whole(others, send_1, recv_1, (0, 0)).wait()
    result = grads[core, spot].astype(F32)
    for k in range(1, 2 * plane_size):
        result = result + part_1[k].astype(F32)
    part_2[z] = result.astype(BF16)
    copies_2 = [
        send(part_2.at[z], part_2.at[z], send_2, recv_2, (0, 0), rows_z[k - 1]) for k in order_z
    ]
    for copy in copies_2:
        copy.start()
    octant_far.wait_recv()
    octant_relay.start()
    lax.fori_loop(0, 4, collect_near, 0)
    whole(far_in, ret_s, ret_r, (0, 0)).wait()

    def final(i, carry):
        cols = [hidden_grad[i, :, c * 128 : c * 128 + 128] for c in range(8)]
        for c in range(8):
            final_taps[0:64, c * 128 : c * 128 + 128] = cols[c]
        for d in range(6):
            face = near[d, i]
            if d < 4:
                face = face + far_in[d, i].astype(F32)
            moved = (shift_plus if d % 2 == 0 else shift_minus)(cols, d // 2, face.astype(BF16))
            for c in range(8):
                final_taps[64 * (d + 1) : 64 * (d + 2), c * 128 : c * 128 + 128] = moved[c]
        values = dot(turned[...], final_taps[...], 1, 0)
        keep_a = flag(counts[0] - 2 * i) > 0
        keep_b = flag(counts[0] - 2 * i) > 1
        for pq in range(4):
            even = values[:, pq * 256 : pq * 256 + 128]
            odd = values[:, pq * 256 + 128 : pq * 256 + 256]
            a = jnp.where(low_half, even, roll(odd, 64))
            b = jnp.where(low_half, roll(even, 64), odd)
            spread = slice(pq * 128, pq * 128 + 128)
            out[2 * i, :, spread] = jnp.where(keep_a, a, 0.0).astype(BF16)
            out[2 * i + 1, :, spread] = jnp.where(keep_b, b, 0.0).astype(BF16)
        return carry

    lax.fori_loop(0, 4, final, 0, unroll=True)
    whole(part_2.at[pl.ds(0, nz - 1)], send_2, recv_2, (0, 0)).wait()
    result = part_2[0].astype(F32)
    for k in range(1, nz):
        result = result + part_2[k].astype(F32)
    part_3[...] = result.astype(BF16)
    hear(3)
    copies_3 = [
        send(part_3, total.at[core, spot], send_3, recv_3, (0, 0), device)
        for _, _, device, _, _ in flat
    ]
    for copy in copies_3:
        copy.start()
    total[core, spot] = result.astype(BF16)
    octant_far.wait_send()
    octant_mate.wait()
    octant_relay.wait()
    for k in range(8):
        coarse[k * 64 : k * 64 + 64, :] = merged_row(maps[0, k], octants, received)
    values = coarse[...].astype(F32)
    active = (values * sigmoid(values)).astype(BF16)
    latent[...] = dot(active, head[...], 1, 1).astype(BF16)
    whole(others, send_3, recv_3, (0, 0)).wait()


def unpack_kernel(
    latent, features, total, latent_out, features_out, conv_out, down_out, head_out,
    conv_hold, down_hold, head_hold, store_s,
):
    scale = float(2048) ** -0.5
    moves = [(features, features_out), (latent, latent_out.at[0])]
    moves += [(conv_hold, conv_out), (down_hold, down_out), (head_hold, head_out)]
    stores = [
        pltpu.make_async_copy(source, target, store_s.at[k])
        for k, (source, target) in enumerate(moves)
    ]
    stores[0].start()
    stores[1].start()
    rows = total[...].reshape(GRAD_ROWS, 128)

    def scaled(first, last):
        return rows[first:last].astype(F32) * scale

    for j in range(4):
        down_hold[:, j * 128 : j * 128 + 128] = scaled(256 + j * 128, 384 + j * 128)
    stores[3].start()
    for j in range(3):
        conv_hold[:, j * 128 : j * 128 + 128] = scaled(j * 64, j * 64 + 64)
    conv_hold[:, 384:448] = scaled(192, 256)[:, :64]
    stores[2].start()
    head_hold[...] = scaled(768, 896)
    stores[4].start()
    for store in stores:
        store.wait()


VM = pl.BlockSpec(memory_space=pltpu.VMEM)
SM = pl.BlockSpec(memory_space=pltpu.SMEM)
ANY = pl.BlockSpec(memory_space=pl.ANY)
HBM = pl.BlockSpec(memory_space=pltpu.HBM)
DMA = pltpu.SemaphoreType.DMA
VMEM = pltpu.VMEM


def shape(*dims, dtype=BF16):
    return jax.ShapeDtypeStruct(dims, dtype)


def bind(kernel, *fixed):
    def run(*refs):
        kernel(*fixed, *refs)

    return run


def body(
    features, neighbours, counts, conv_weight, down_weight, head_weight, coarse_map, latent_grad
):
    n_gx, n_gy = lax.axis_size("gx"), lax.axis_size("gy")
    nz = ring_z(n_gx)
    spots = (n_gx // nz) * (n_gy // 2)
    per = GRAD_ROWS // 2 // spots
    latent, grad, total = pl.pallas_call(
        bind(step_kernel, n_gx, n_gy), name="step", in_specs=[SM] + [HBM] * 7,
        out_specs=[VM] * 3,
        out_shape=[shape(512, 128), shape(8, 64, 512), shape(2, spots, per, 128)],
        scratch_shapes=[
            pltpu.SMEM((8, 6), jnp.int32), pltpu.SMEM((1, 8), jnp.int32),
            VMEM((64, 448), BF16), VMEM((128, 512), BF16), VMEM((128, 128), BF16),
            VMEM((8, 64, 512), BF16), VMEM((8, 64, 128), BF16), VMEM((24, 64, 128), BF16),
            VMEM((8, 128), jnp.int32), VMEM((3, 8, 128), jnp.int32),
            VMEM((512, 128), BF16), VMEM((64, 448), BF16), VMEM((4, 9, 64, 128), BF16), VMEM((2, 9, 64, 128), BF16),
            VMEM((4, 448, 1024), BF16), VMEM((4, 64, 1024), F32), VMEM((4, 512, 128), BF16),
            VMEM((8, 64, 128), BF16), VMEM((24, 64, 128), BF16),
            pltpu.SMEM((8,), jnp.int32), VMEM((4, 64, 1024), BF16), VMEM((6, 2, 4, 64, 128), F32),
            VMEM((6, 4, 64, 128), F32), VMEM((4, 4, 64, 128), BF16), VMEM((4, 4, 64, 128), BF16),
            VMEM((64, 448), F32), VMEM((512, 128), F32), VMEM((128, 128), F32),
            VMEM((448, 1024), BF16), VMEM((512, 128), BF16),
            VMEM((2, spots, per, 128), BF16), VMEM((2 * spots, per, 128), BF16),
            VMEM((nz, per, 128), BF16), VMEM((per, 128), BF16),
            pltpu.SemaphoreType.REGULAR((4,)), DMA((10,)),
            DMA((2,)), DMA((2,)), DMA((3,)), DMA((3,)), DMA((3,)), DMA((6,)),
            DMA((1,)), DMA((1,)), DMA((1,)), DMA((1,)), DMA((1,)), DMA((1,)), DMA((1,)), DMA((1,)),
        ],
        compiler_params=pltpu.CompilerParams(
            collective_id=0, has_side_effects=True, vmem_limit_bytes=20 * 2**20,
        ),
    )(
        counts, *[
            pltpu.with_memory_space_constraint(value, pltpu.HBM)
            for value in (
                neighbours, coarse_map, conv_weight, down_weight, head_weight, features,
                latent_grad.reshape(8, 64, 128),
            )
        ],
    )
    return pl.pallas_call(
        unpack_kernel, name="unpack", in_specs=[VM] * 3, out_specs=[ANY] * 5,
        out_shape=[
            shape(1, 512, 128), shape(8, 64, 512), shape(64, 448, dtype=F32),
            shape(128, 512, dtype=F32), shape(128, 128, dtype=F32),
        ],
        scratch_shapes=[
            VMEM((64, 448), F32), VMEM((128, 512), F32), VMEM((128, 128), F32), DMA((5,)),
        ],
        compiler_params=pltpu.CompilerParams(vmem_limit_bytes=8 * 2**20),
    )(latent, grad, total)


def solution(mesh):
    placed = (
        P(("gx", "gy"), None, None),
        P(("gx", "gy"), None),
        P(("gx", "gy")),
        P(),
        P(),
        P(),
        P(("gx", "gy"), None),
        P(("gx", "gy"), None, None),
    )
    return jax.shard_map(
        body,
        mesh=mesh,
        in_specs=placed,
        out_specs=(P(("gx", "gy"), None, None), P(("gx", "gy"), None, None), P(), P(), P()),
        check_vma=False,
    )
```
